256 devices in a mesh: tm: 32 (over x_lo, z, core), rows: 8 (over y, x_hi).
Axes of the slice: x: 4 (x_hi: 2, x_lo: 2; x = x_hi * 2 + x_lo), y: 4, z: 8, core: 2. Of those that a mesh axis runs over, the one named last changes fastest.
Arguments:
- video: bfloat16 [64, 16, 64, 384], P('tm', 'rows'), may hold values from -6 to 6
- conv_weight: bfloat16 [3, 3, 3, 384, 384], replicated, may hold values from -0.0625 to 0.0625
- norm_gain: float32 [384], replicated, may hold values from 0.1 to 1.9
- w_query: bfloat16 [384, 384], replicated, may hold values from -0.3125 to 0.3125
- w_key: bfloat16 [384, 384], replicated, may hold values from -0.875 to 0.875
- w_value: bfloat16 [384, 384], replicated, may hold values from -0.875 to 0.875
- w_out: bfloat16 [384, 384], replicated, may hold values from -0.3125 to 0.3125
- cotangent: bfloat16 [64, 16, 64, 384], P('tm', 'rows'), may hold values from -6 to 6
Outputs:
- block_out: bfloat16 [64, 16, 64, 384], P('tm', 'rows')
- video_grad: bfloat16 [64, 16, 64, 384], P('tm', 'rows')
The draws below stay inside these ranges and needn't reach their ends.
All inputs are finite; a program needn't handle non-finite values.
Results may differ from the reference program's by a relative error of at most 0.014.
Values may be sent and summed in bfloat16 or wider, within the bound.
No kernel may reach another device: no remote copies, remote signals or barrier semaphores. Data moves between devices by JAX's collectives and lax.ppermute only.
A program may use at most 64 MiB of HBM per device.

```python
import jax
import jax.numpy as jnp
from jax import lax

CHANNELS = 384
WIDTH = 64
FRAMES = 64
HEIGHT = 16


def block_scale(key, extent, split, smallest, top_value):
    def one(axis_at, shards_of):
        steps = jax.random.uniform(jax.random.fold_in(jax.random.fold_in(key, 6), axis_at), (shards_of,), jnp.float32, smallest / len(split), top_value / len(split))
        return jnp.repeat(jnp.exp(steps), extent[axis_at] // shards_of).reshape((-1,) + (1,) * (len(extent) - axis_at - 1))

    factor_of = one(*split[0])
    for cut in split[1:]:
        factor_of = factor_of * one(*cut)
    return factor_of


def noise(key, dims, scale, most, shards=(), held_as=jnp.bfloat16):
    entries = scale * jax.random.normal(key, dims, jnp.float32)
    if shards:
        entries = entries * block_scale(key, dims, shards, -0.22, 0.18)
    return jnp.clip(entries, -most, most).astype(held_as)


def setup_inputs(seed: int = 0) -> dict:
    splits = jax.random.split(jax.random.key(seed), 9)
    return {
        "video": noise(splits[0], (FRAMES, HEIGHT, WIDTH, CHANNELS), 1.0, 6.0, ((0, 32), (1, 8))),
        "conv_weight": noise(splits[1], (3, 3, 3, CHANNELS, CHANNELS), (27 * CHANNELS) ** -0.5, 0.0625),
        "norm_gain": jnp.clip(1.0 + 0.18 * jax.random.normal(splits[2], (CHANNELS,), jnp.float32), 0.1, 1.9),
        "w_query": noise(splits[3], (CHANNELS, CHANNELS), CHANNELS ** -0.5, 0.3125),
        "w_key": noise(splits[4], (CHANNELS, CHANNELS), (CHANNELS // 8) ** -0.5, 0.875),
        "w_value": noise(splits[5], (CHANNELS, CHANNELS), (CHANNELS // 8) ** -0.5, 0.875),
        "w_out": noise(splits[6], (CHANNELS, CHANNELS), CHANNELS ** -0.5, 0.3125),
        "cotangent": noise(splits[7], (FRAMES, HEIGHT, WIDTH, CHANNELS), 1.0, 6.0, ((0, 32), (1, 8))),
    }


def convolve(padded, kernel, pads):
    result = lax.conv_general_dilated(padded[None], kernel, (1, 1, 1), pads, dimension_numbers=('NDHWC', 'DHWIO', 'NDHWC'), preferred_element_type=jnp.float32)
    return result[0]

def reference(video, conv_weight, norm_gain, w_query, w_key, w_value, w_out, cotangent):
    chans = video.shape[3]
    scale = 1.0 / jnp.sqrt(jnp.float32(chans))
    padded = jnp.pad(video, ((2, 0), (1, 1), (1, 1), (0, 0)))
    conv = convolve(padded, conv_weight, [(0, 0), (0, 0), (0, 0)]).astype(jnp.bfloat16)
    convf = conv.astype(jnp.float32)
    inverse = lax.rsqrt(lax.optimization_barrier(jnp.mean(convf * convf, axis=-1, keepdims=True)) + 1e-06)
    normed = convf * inverse * norm_gain
    act = jax.nn.silu(normed).astype(jnp.bfloat16)
    frames = video.shape[0]
    flat = act.reshape(-1, chans)
    queries = jnp.dot(flat, w_query, preferred_element_type=jnp.float32).astype(jnp.bfloat16).reshape(frames, -1, chans)
    keys = jnp.dot(flat, w_key, preferred_element_type=jnp.float32).astype(jnp.bfloat16).reshape(frames, -1, chans)
    values = jnp.dot(flat, w_value, preferred_element_type=jnp.float32).astype(jnp.bfloat16).reshape(frames, -1, chans)

    def forward_frame(items):
        query_f, key_f, value_f = items
        scores = jnp.dot(query_f, key_f.T, preferred_element_type=jnp.float32) * scale
        top = lax.optimization_barrier(jnp.max(scores, axis=-1, keepdims=True))
        expo = jnp.exp(scores - top)
        total = lax.optimization_barrier(jnp.sum(expo, axis=-1, keepdims=True))
        probs = expo / total
        attended = jnp.dot(probs.astype(jnp.bfloat16), value_f, preferred_element_type=jnp.float32).astype(jnp.bfloat16)
        return (attended, (top + jnp.log(total))[:, 0])
    attended, logsum = lax.map(forward_frame, (queries, keys, values))
    projected = jnp.dot(attended.reshape(-1, chans), w_out, preferred_element_type=jnp.float32)
    block_out = (act.astype(jnp.float32).reshape(-1, chans) + projected).astype(jnp.bfloat16).reshape(video.shape)
    grad_att = jnp.dot(cotangent.reshape(-1, chans), w_out.T, preferred_element_type=jnp.float32).astype(jnp.bfloat16).reshape(frames, -1, chans)

    def backward_frame(items):
        query_f, key_f, value_f, attended_f, grad_f, logsum_f = items
        scores = jnp.dot(query_f, key_f.T, preferred_element_type=jnp.float32) * scale
        probs = jnp.exp(scores - logsum_f[:, None])
        delta = lax.optimization_barrier(jnp.sum(grad_f.astype(jnp.float32) * attended_f.astype(jnp.float32), axis=-1))
        dprob = jnp.dot(grad_f, value_f.T, preferred_element_type=jnp.float32)
        dscore = (probs * (dprob - delta[:, None])).astype(jnp.bfloat16)
        grad_q = (jnp.dot(dscore, key_f, preferred_element_type=jnp.float32) * scale).astype(jnp.bfloat16)
        grad_k = (jnp.dot(dscore.T, query_f, preferred_element_type=jnp.float32) * scale).astype(jnp.bfloat16)
        grad_v = jnp.dot(probs.astype(jnp.bfloat16).T, grad_f, preferred_element_type=jnp.float32).astype(jnp.bfloat16)
        return (grad_q, grad_k, grad_v)
    grad_q, grad_k, grad_v = lax.map(backward_frame, (queries, keys, values, attended, grad_att, logsum))
    grad_act = cotangent.astype(jnp.float32).reshape(-1, chans)
    grad_act = grad_act + jnp.dot(grad_q.reshape(-1, chans), w_query.T, preferred_element_type=jnp.float32)
    grad_act = grad_act + jnp.dot(grad_k.reshape(-1, chans), w_key.T, preferred_element_type=jnp.float32)
    grad_act = grad_act + jnp.dot(grad_v.reshape(-1, chans), w_value.T, preferred_element_type=jnp.float32)
    grad_act = grad_act.reshape(video.shape)
    sigma = jax.nn.sigmoid(normed)
    grad_normed = grad_act * sigma * (1.0 + normed * (1.0 - sigma))
    scaled = grad_normed * norm_gain
    grad_conv = inverse * (scaled - convf * inverse * inverse * lax.optimization_barrier(jnp.mean(scaled * convf, axis=-1, keepdims=True)))
    grad_conv = grad_conv.astype(jnp.bfloat16)
    flipped = jnp.transpose(jnp.flip(conv_weight, (0, 1, 2)), (0, 1, 2, 4, 3))
    grad_padded = convolve(grad_conv, flipped, [(2, 2), (2, 2), (1, 1)])
    video_grad = grad_padded[2:, 1:-1].astype(jnp.bfloat16)
    return (block_out, video_grad)
```

```python
import functools

import jax
import jax.numpy as jnp
from jax import lax
from jax.experimental import pallas as pl
from jax.experimental.pallas import tpu as pltpu
from jax.sharding import PartitionSpec as P


F32 = jnp.float32
BF16 = jnp.bfloat16
VMEM_LIMIT = 40 * 1024 * 1024


def full(shape):
    zeros = (0,) * len(shape)
    return pl.BlockSpec(shape, lambda b, zeros=zeros: zeros)


def spread(rows_f32, width):
    n = rows_f32.shape[0]
    col = lax.broadcasted_iota(jnp.int32, rows_f32.shape, 0) % width
    left = jnp.where(col == 0, 0.0, pltpu.roll(rows_f32, 1, 0))
    right = jnp.where(col == width - 1, 0.0, pltpu.roll(rows_f32, n - 1, 0))
    return left, rows_f32, right


def fill(taps, frame, row, block, width, flip):
    n, _, chans = block.shape
    shifted = spread(block.astype(F32).reshape(n * width, chans), width)
    if flip:
        shifted = shifted[::-1]
    for c in range(3):
        taps[frame, pl.ds(row, n), :, c * chans : (c + 1) * chans] = (
            shifted[c].astype(BF16).reshape(n, width, chans)
        )


def gathered(taps, frame, row):
    piece = taps[frame, pl.ds(row, 2)]
    return piece.reshape(piece.shape[0] * piece.shape[1], piece.shape[2])


def conv_steps(taps, w_main, w_side, acc, out, src, dst, transposed):
    b = pl.program_id(0)
    row = (2 - b) if transposed else b

    def times(lhs, w_ref):
        chans = w_ref.shape[-1]
        if not transposed:
            return jnp.dot(lhs, w_ref[...].reshape(3 * chans, chans), preferred_element_type=F32)
        total = None
        for c in range(3):
            term = lax.dot_general(
                lhs[:, c * chans : (c + 1) * chans],
                w_ref[c],
                (((1,), (1,)), ((), ())),
                preferred_element_type=F32,
            )
            total = term if total is None else total + term
        return total

    lhs = [gathered(taps, f, row) for f in range(2)]
    main = times(jnp.concatenate(lhs, axis=0), w_main)
    side = times(lhs[src], w_side)
    half = main.shape[0] // 2
    for f in range(2):
        term = main[f * half : (f + 1) * half]
        if f == dst:
            term = term + side

        @pl.when(b == 0)
        def _(term=term, f=f):
            acc[f] = term

        @pl.when(b > 0)
        def _(term=term, f=f):
            acc[f] += term

    @pl.when(b == 2)
    def _():
        out[...] = acc[...].astype(out.dtype)


def forward_kernel(src, dst, up, mid, down, w_main, w_side, out, taps, acc):
    width = mid.shape[2]

    @pl.when(pl.program_id(0) == 0)
    def _():
        for f in range(2):
            fill(taps, f, 0, up[f], width, False)
            fill(taps, f, 1, mid[f], width, False)
            fill(taps, f, 3, down[f], width, False)

    conv_steps(taps, w_main, w_side, acc, out, src, dst, False)


def backward_kernel(src, dst, x_ref, r0, r1, h0, h1, w_main, w_side, out, taps, acc):
    width = r0.shape[1]

    @pl.when(pl.program_id(0) == 0)
    def _():
        x = x_ref[0]
        fill(taps, x, 1 - x, r0[...], width, True)
        fill(taps, 1 - x, 1 - x, r1[...], width, True)
        fill(taps, x, 3 * x, h0[...], width, True)
        fill(taps, 1 - x, 3 * x, h1[...], width, True)

    conv_steps(taps, w_main, w_side, acc, out, src, dst, True)


def conv_call(kernel, operands, scalars, weight, main, side, dtype, name):
    width, chans = operands[0].shape[-2:]
    taps_w = (None, None, 3, chans, chans)
    return pl.pallas_call(
        kernel,
        grid=(3,),
        in_specs=[pl.BlockSpec(memory_space=pltpu.SMEM) for _ in scalars]
        + [full(o.shape) for o in operands]
        + [
            pl.BlockSpec(taps_w, lambda b: (main, b, 0, 0, 0)),
            pl.BlockSpec(taps_w, lambda b: (side, b, 0, 0, 0)),
        ],
        out_specs=full((2, 2 * width, chans)),
        out_shape=jax.ShapeDtypeStruct((2, 2 * width, chans), dtype),
        scratch_shapes=[
            pltpu.VMEM((2, 4, width, 3 * chans), BF16),
            pltpu.VMEM((2, 2 * width, chans), F32),
        ],
        compiler_params=pltpu.CompilerParams(vmem_limit_bytes=VMEM_LIMIT),
        cost_estimate=pl.CostEstimate(
            flops=2 * 9 * 3 * 128 * chans * chans,
            bytes_accessed=18 * chans * chans * 2,
            transcendentals=0,
        ),
        name=name,
    )(*scalars, *operands, weight, weight)


def norm_parts(conv, gain):
    convf = conv.astype(F32)
    inverse = lax.rsqrt(jnp.mean(convf * convf, axis=-1, keepdims=True) + 1e-06)
    normed = convf * inverse * gain
    return convf, inverse, normed


def mm(a, b):
    return jnp.dot(a, b, preferred_element_type=F32)


def mm_t(a, b):
    return lax.dot_general(a, b, (((1,), (1,)), ((), ())), preferred_element_type=F32)


def t_mm(a, b):
    return lax.dot_general(a, b, (((0,), (0,)), ((), ())), preferred_element_type=F32)


def attention_kernel(
    x_ref, c00, c01, c10, c11, cs, t00, t01, t10, t11, ts, gain_ref, wq, wk, wv, wo,
    out, gout, conv_s, cot_s, act_s, q_s, k_s, v_s, g_s, gk_s, gv_s,
):
    x = x_ref[0]
    block = c00.shape[0]
    own = 2 * block
    chans = wq.shape[0]
    scale = 1.0 / jnp.sqrt(jnp.float32(chans))
    gain = gain_ref[...]
    lo = pl.multiple_of(x * block, block)
    hi = pl.multiple_of((1 - x) * block, block)
    for dst, pieces in ((conv_s, (c00, c01, c10, c11, cs)), (cot_s, (t00, t01, t10, t11, ts))):
        dst[pl.ds(lo, block)] = pieces[0][...]
        dst[pl.ds(hi, block)] = pieces[1][...]
        dst[own : own + block] = pieces[2][...]
        dst[own + block : 2 * own] = pieces[3][...]
        dst[2 * own :] = pieces[4][...]
    chunks = conv_s.shape[0] // own
    for i in range(chunks):
        rows = slice(i * own, (i + 1) * own)
        _, _, normed = norm_parts(conv_s[rows], gain)
        act = (normed / (1.0 + jnp.exp(-normed))).astype(BF16)
        if i == 0:
            act_s[...] = act
        q_s[rows] = mm(act, wq[...]).astype(BF16)
        k_s[rows] = mm(act, wk[...]).astype(BF16)
        v_s[rows] = mm(act, wv[...]).astype(BF16)
        g_s[rows] = mm_t(cot_s[rows], wo[...]).astype(BF16)
    attended = grad_q = None
    for i in range(chunks):
        rows = slice(i * own, (i + 1) * own)
        scores = mm_t(q_s[rows], k_s[...]) * scale
        top = jnp.max(scores, axis=-1, keepdims=True)
        expo = jnp.exp(scores - top)
        inv_total = 1.0 / jnp.sum(expo, axis=-1, keepdims=True)
        dprob = mm_t(g_s[rows], v_s[...])
        delta = jnp.sum(expo * dprob, axis=-1, keepdims=True) * inv_total
        if i == 0:
            probs = expo * inv_total
            probs_b = probs.astype(BF16)
            attended = mm(probs_b, v_s[...]).astype(BF16)
            dscore = (probs * (dprob - delta)).astype(BF16)
            grad_q = (mm(dscore, k_s[...]) * scale).astype(BF16)
            gk_s[...] = t_mm(dscore[:, :own], q_s[rows])
            gv_s[...] = t_mm(probs_b[:, :own], g_s[rows])
        else:
            probs = expo[:, :own] * inv_total
            dscore = (probs * (dprob[:, :own] - delta)).astype(BF16)
            gk_s[...] += t_mm(dscore, q_s[rows])
            gv_s[...] += t_mm(probs.astype(BF16), g_s[rows])
    out[...] = (act_s[...].astype(F32) + mm(attended, wo[...])).astype(BF16)
    grad_act = cot_s[:own].astype(F32)
    grad_act = grad_act + mm_t(grad_q, wq[...])
    grad_act = grad_act + mm_t((gk_s[...] * scale).astype(BF16), wk[...])
    grad_act = grad_act + mm_t(gv_s[...].astype(BF16), wv[...])
    convf, inverse, normed = norm_parts(conv_s[:own], gain)
    sigma = 1.0 / (1.0 + jnp.exp(-normed))
    scaled = grad_act * sigma * (1.0 + normed * (1.0 - sigma)) * gain
    mean = jnp.mean(scaled * convf, axis=-1, keepdims=True)
    gout[...] = (inverse * (scaled - convf * inverse * inverse * mean)).astype(BF16)


def attention(x, convs, cots, gain, wq, wk, wv, wo):
    block, chans = convs[0].shape
    own, whole = 2 * block, 8 * block
    vm = pl.BlockSpec(memory_space=pltpu.VMEM)
    act = lambda n, t=BF16: pltpu.VMEM((n, chans), t)
    return pl.pallas_call(
        attention_kernel,
        in_specs=[pl.BlockSpec(memory_space=pltpu.SMEM)] + [vm] * 15,
        out_specs=[vm, vm],
        out_shape=[jax.ShapeDtypeStruct((own, chans), BF16)] * 2,
        scratch_shapes=[act(whole), act(whole), act(own)]
        + [act(whole)] * 4
        + [act(own, F32), act(own, F32)],
        compiler_params=pltpu.CompilerParams(vmem_limit_bytes=VMEM_LIMIT),
        cost_estimate=pl.CostEstimate(
            flops=4 * 10**9, bytes_accessed=4 * 10**6, transcendentals=1 << 20
        ),
        name="attention",
    )(x, *convs, *cots, gain, wq, wk, wv, wo)


def sites(runs):
    for h in range(runs // 2):
        for c in range(2):
            for y in range(4):
                for x in range(2):
                    yield h, c, y, x


def site(h, c, y, x):
    return (h * 2 + c) * 8 + 2 * y + x


def spread_pairs(runs, ky, kx):
    return [
        (site(h, c, y, x), site(h, y % 2, 2 * ((y // 2 + ky) % 2) + c, x ^ kx))
        for h, c, y, x in sites(runs)
    ]


def return_pairs(runs, kx):
    return [
        (site(h, c, y, x), site(h, y % 2, 2 * (y // 2) + c, x ^ kx)) for h, c, y, x in sites(runs)
    ]


def rim_pairs(runs, kx):
    pairs = []
    for h, c, y, x in sites(runs):
        to_x = x ^ kx
        to_y = 2 * (y // 2) + c + (1 if to_x == 0 else -1)
        if 0 <= to_y < 4:
            pairs.append((site(h, c, y, x), site(h, y % 2, to_y, to_x)))
    return pairs


BOTH = ("tm", "rows")


def to_frames(value, x, runs):
    same = lax.dynamic_index_in_dim(value, x, 0, keepdims=False)
    other = lax.dynamic_index_in_dim(value, 1 - x, 0, keepdims=False)
    got = {}
    for ky in (1, 0):
        for kx in (1, 0):
            got[ky, kx] = lax.ppermute(
                other if kx else same, BOTH, spread_pairs(runs, ky, kx)
            )
    blocks = [got[0, 0], got[0, 1], got[1, 0], got[1, 1]]
    swapped = lax.ppermute(
        jnp.concatenate(blocks, axis=0), "tm", [(i, i ^ 1) for i in range(runs)]
    )
    return blocks + [swapped]


def local(video, conv_weight, norm_gain, w_query, w_key, w_value, w_out, cotangent):
    frames, height, width, chans = video.shape
    runs, slabs = lax.axis_size("tm"), lax.axis_size("rows")
    assert (frames, height, slabs) == (2, 2, 8)
    x = lax.axis_index("rows") % 2
    x_arg = jnp.reshape(x, (1,)).astype(jnp.int32)

    up = lax.ppermute(video[:, 1:], "rows", [(i, i + 1) for i in range(slabs - 1)])
    down = lax.ppermute(video[:, :1], "rows", [(i + 1, i) for i in range(slabs - 1)])
    cots = to_frames(cotangent.reshape(2, 2 * width, chans), x, runs)

    slab = (up, video, down)
    for_next = conv_call(
        functools.partial(forward_kernel, 1, 0), slab, (), conv_weight, 0, 1, BF16, "conv_next"
    )
    cached = lax.ppermute(for_next, "tm", [(i, i + 1) for i in range(runs - 1)])
    own = conv_call(
        functools.partial(forward_kernel, 0, 1), slab, (), conv_weight, 2, 1, F32, "conv_own"
    )
    conv = (own + cached.astype(F32)).astype(BF16)
    convs = to_frames(conv, x, runs)

    out, grad_conv = attention(
        x_arg, convs, cots, norm_gain.reshape(1, chans), w_query, w_key, w_value, w_out
    )
    out = out.reshape(4, width, chans)
    grad_conv = grad_conv.reshape(4, width, chans)

    returned, rims, outs = [], [], []
    for kx in (0, 1):
        to_x = jnp.where(kx == 0, x, 1 - x)
        rows = lax.dynamic_slice_in_dim(grad_conv, to_x, 3, 0)
        returned.append(lax.ppermute(rows, BOTH, return_pairs(runs, kx)))
        rim = lax.dynamic_slice_in_dim(grad_conv, 3 * (1 - to_x), 1, 0)
        rims.append(lax.ppermute(rim, BOTH, rim_pairs(runs, kx)))
    for kx in (0, 1):
        to_x = jnp.where(kx == 0, x, 1 - x)
        rows = lax.dynamic_slice_in_dim(out, 2 * to_x, 2, 0)
        outs.append(lax.ppermute(rows, BOTH, return_pairs(runs, kx)))

    slab = (*returned, *rims)
    for_last = conv_call(
        functools.partial(backward_kernel, 0, 1), slab, (x_arg,), conv_weight, 0, 1, BF16, "grad_last"
    )
    handed = lax.ppermute(for_last, "tm", [(i + 1, i) for i in range(runs - 1)])
    own_grad = conv_call(
        functools.partial(backward_kernel, 1, 0), slab, (x_arg,), conv_weight, 2, 1, F32, "grad_own"
    )
    video_grad = (own_grad + handed.astype(F32)).astype(BF16).reshape(video.shape)
    block_out = jnp.where(x == 0, jnp.stack(outs), jnp.stack(outs[::-1]))
    return (block_out, video_grad)


def solution(mesh):
    spec = P("tm", "rows", None, None)
    return jax.shard_map(
        local,
        mesh=mesh,
        in_specs=(spec, P(), P(), P(), P(), P(), P(), spec),
        out_specs=(spec, spec),
        check_vma=False,
    )
```

```python
import functools

import jax
import jax.numpy as jnp
from jax import lax
from jax.experimental import pallas as pl
from jax.experimental.pallas import tpu as pltpu
from jax.sharding import PartitionSpec as P


F32 = jnp.float32
BF16 = jnp.bfloat16
MIB = 1024 * 1024
LOAD = 42 * MIB
PREPARE = 533 * MIB // 10
VM = pl.BlockSpec(memory_space=pltpu.VMEM)
SM = pl.BlockSpec(memory_space=pltpu.SMEM)
HBM = pl.BlockSpec(memory_space=pltpu.HBM)


def call(kernel, operands, specs, shapes, scratch, limit, cost=0):
    return pl.pallas_call(
        kernel,
        in_specs=specs,
        out_specs=[VM] * len(shapes),
        out_shape=[jax.ShapeDtypeStruct(dims, dtype) for dims, dtype in shapes],
        scratch_shapes=scratch,
        compiler_params=pltpu.CompilerParams(vmem_limit_bytes=limit),
        cost_estimate=pl.CostEstimate(flops=cost, bytes_accessed=1 << 20, transcendentals=0),
    )(*operands)


def prepare_kernel(place, video, cot, packet, far, same, held, sems):
    x = place[0]
    width = far.shape[0] // 2
    moves = [
        (cot.at[1 - x], packet.at[2 * width :]),
        (cot.at[x], same),
        (video, held),
    ]
    for f in range(2):
        moves.append((video.at[f, 1 - x], packet.at[f * width : (f + 1) * width]))
        moves.append((video.at[f, x], far.at[f * width : (f + 1) * width]))
    copies = [pltpu.make_async_copy(a, b, sems.at[i]) for i, (a, b) in enumerate(moves)]
    for copy in copies:
        copy.start()
    for copy in copies:
        copy.wait()


def prepare(place, video, cot):
    _, _, width, chans = video.shape
    return call(
        prepare_kernel, (place, video, cot), [SM, HBM, HBM],
        [((4 * width, chans), BF16), ((2 * width, chans), BF16), (cot.shape[1:], BF16), (video.shape, BF16)],
        [pltpu.SemaphoreType.DMA((7,))], PREPARE,
    )


def join_kernel(same, packet, out):
    half = same.shape[0]
    out[:half] = same[...]
    out[half:] = packet[half:]


def join(same, packet):
    return call(join_kernel, (same, packet), [VM, VM], [(packet.shape, BF16)], [], 4 * MIB)[0]


def merge_kernel(place, own, cached, same, other):
    x = place[0]
    same[...] = (own[x] + cached[x].astype(F32)).astype(BF16)
    other[...] = (own[1 - x] + cached[1 - x].astype(F32)).astype(BF16)


def merge(place, own, cached):
    return call(merge_kernel, (place, own, cached), [SM, VM, VM], [(own.shape[1:], BF16)] * 2, [], 8 * MIB)


def load_kernel(w_hbm, w_out, sem):
    copy = pltpu.make_async_copy(w_hbm, w_out, sem)
    copy.start()
    copy.wait()


def load(weight):
    return call(load_kernel, (weight,), [HBM], [(weight.shape, BF16)], [pltpu.SemaphoreType.DMA], LOAD)[0]


def finish_kernel(place, out0, out1, own, handed, block_out, video_grad, total, sems):
    x = place[0]
    copies = [
        pltpu.make_async_copy(out0, block_out.at[x], sems.at[0]),
        pltpu.make_async_copy(out1, block_out.at[1 - x], sems.at[1]),
    ]
    for copy in copies:
        copy.start()
    total[...] = (own[...] + handed[...].astype(F32)).astype(BF16)
    copies.append(pltpu.make_async_copy(total, video_grad, sems.at[2]))
    copies[2].start()
    for copy in copies:
        copy.wait()


def finish(place, out0, out1, own, handed):
    return pl.pallas_call(
        finish_kernel,
        in_specs=[SM] + [VM] * 4,
        out_specs=[HBM, HBM],
        out_shape=[
            jax.ShapeDtypeStruct((2,) + out0.shape, BF16),
            jax.ShapeDtypeStruct(own.shape, BF16),
        ],
        scratch_shapes=[pltpu.VMEM(own.shape, BF16), pltpu.SemaphoreType.DMA((3,))],
        compiler_params=pltpu.CompilerParams(vmem_limit_bytes=8 * MIB),
        name="finish",
    )(place, out0, out1, own, handed)


def spread(rows_f32, width):
    n = rows_f32.shape[0]
    col = lax.broadcasted_iota(jnp.int32, rows_f32.shape, 0) % width
    left = jnp.where(col == 0, 0.0, pltpu.roll(rows_f32, 1, 0))
    right = jnp.where(col == width - 1, 0.0, pltpu.roll(rows_f32, n - 1, 0))
    return left, rows_f32, right


def fill(taps, frame, row, block, width, flip):
    n, _, chans = block.shape
    shifted = spread(block.astype(F32).reshape(n * width, chans), width)
    if flip:
        shifted = shifted[::-1]
    for c in range(3):
        taps[frame, pl.ds(row, n), :, c * chans : (c + 1) * chans] = (
            shifted[c].astype(BF16).reshape(n, width, chans)
        )


def conv_steps(taps, w_ref, main, side, out, src, dst, transposed):
    chans = w_ref.shape[-1]

    def times(lhs, a, b):
        if not transposed:
            return mm(lhs, w_ref[a, b].reshape(3 * chans, chans))
        return mm_t(lhs, jnp.concatenate([w_ref[a, b, c] for c in range(3)], axis=1))

    both = extra = None
    for b in range(3):
        row = (2 - b) if transposed else b
        lhs = [taps[f, row : row + 2] for f in range(2)]
        lhs = [v.reshape(v.shape[0] * v.shape[1], v.shape[2]) for v in lhs]
        term = times(jnp.concatenate(lhs, axis=0), main, b)
        both = term if both is None else both + term
        term = times(lhs[src], side, b)
        extra = term if extra is None else extra + term
    half = both.shape[0] // 2
    for f in range(2):
        term = both[f * half : (f + 1) * half]
        out[f] = (term + extra if f == dst else term).astype(out.dtype)


def forward_kernel(main, side, src, dst, place, packet, mid, far, w_ref, out, taps):
    width, chans = mid.shape[2:]
    x = place[0]
    for f in range(2):
        line = slice(f * width, (f + 1) * width)
        fill(taps, f, 3 * (1 - x), packet[line].reshape(1, width, chans), width, False)
        fill(taps, f, 1, mid[f], width, False)
        fill(taps, f, 3 * x, far[line].reshape(1, width, chans), width, False)
    conv_steps(taps, w_ref, main, side, out, src, dst, False)


def backward_kernel(main, side, src, dst, place, r0, r1, w_ref, out, taps):
    width, chans = taps.shape[2], w_ref.shape[-1]
    x = place[0]
    fill(taps, x, 0, r0[...].reshape(4, width, chans), width, True)
    fill(taps, 1 - x, 0, r1[...].reshape(4, width, chans), width, True)
    conv_steps(taps, w_ref, main, side, out, src, dst, True)


def conv_call(kernel, place, operands, weight, width, dtype):
    chans = weight.shape[-1]
    return call(
        kernel, (place, *operands, weight), [SM] + [VM] * (len(operands) + 1),
        [((2, 2 * width, chans), dtype)], [pltpu.VMEM((2, 4, width, 3 * chans), BF16)],
        24 * MIB, 2 * 9 * 3 * 128 * chans * chans,
    )[0]


def norm_parts(conv, gain):
    convf = conv.astype(F32)
    inverse = lax.rsqrt(jnp.mean(convf * convf, axis=-1, keepdims=True) + 1e-06)
    normed = convf * inverse * gain
    return convf, inverse, normed


def mm(a, b):
    return jnp.dot(a, b, preferred_element_type=F32)


def mm_t(a, b):
    return lax.dot_general(a, b, (((1,), (1,)), ((), ())), preferred_element_type=F32)


def t_mm(a, b):
    return lax.dot_general(a, b, (((0,), (0,)), ((), ())), preferred_element_type=F32)


CHUNKS = ((0, 384), (384, 256), (640, 256), (896, 128))


def attention_kernel(
    place, c00, c01, c10, c11, s00, s01, s10, s11, t0, t2, u0, u2, gain_ref, wq, wk, wv, wo,
    out0, out1, grad0, grad1, conv_s, cot_s, act_s, q_s, k_s, v_s, g_s, gk_s, gv_s, out_s, grad_s,
):
    x, q = place[0], place[1]
    line = c00.shape[0] // 2
    own = 6 * line
    chans = wq.shape[0]
    scale = 1.0 / jnp.sqrt(jnp.float32(chans))
    gain = gain_ref[...]

    def put(dst, value, quarter, kx):
        for j in range(2):
            slot = (4 * (quarter - q) + 2 * (x + kx - 2 * x * kx) + j + 17) % 16
            dst[pl.ds(pl.multiple_of(slot * line, line), line)] = value[j * line : (j + 1) * line]

    side = q + 1 - 2 * (q % 2)
    far = (q + 2) % 4
    far_side = (side + 2) % 4
    for ref, quarter, kx in (
        (c00, q, 0), (c01, q, 1), (c10, far, 0), (c11, far, 1),
        (s00, side, 0), (s01, side, 1), (s10, far_side, 0), (s11, far_side, 1),
    ):
        put(conv_s, ref, quarter, kx)
    for ref, quarter in ((t0, q), (t2, far), (u0, side), (u2, far_side)):
        for kx in range(2):
            put(cot_s, ref.at[2 * kx * line : 2 * (kx + 1) * line], quarter, kx)

    for at, n in CHUNKS:
        rows = slice(at, at + n)
        _, _, normed = norm_parts(conv_s[rows], gain)
        act = (normed / (1.0 + jnp.exp(-normed))).astype(BF16)
        if at == 0:
            act_s[...] = act
        q_s[rows] = mm(act, wq[...]).astype(BF16)
        k_s[rows] = mm(act, wk[...]).astype(BF16)
        v_s[rows] = mm(act, wv[...]).astype(BF16)
        g_s[rows] = mm_t(cot_s[rows], wo[...]).astype(BF16)
    attended = grad_q = None
    for at, n in CHUNKS:
        rows = slice(at, at + n)
        scores = mm_t(q_s[rows], k_s[...]) * scale
        top = jnp.max(scores, axis=-1, keepdims=True)
        expo = jnp.exp(scores - top)
        inv_total = 1.0 / jnp.sum(expo, axis=-1, keepdims=True)
        dprob = mm_t(g_s[rows], v_s[...])
        delta = jnp.sum(expo * dprob, axis=-1, keepdims=True) * inv_total
        if at == 0:
            probs = expo * inv_total
            probs_b = probs.astype(BF16)
            mid = slice(line, own - line)
            attended = mm(probs_b[mid], v_s[...]).astype(BF16)
            dscore = (probs * (dprob - delta)).astype(BF16)
            grad_q = (mm(dscore, k_s[...]) * scale).astype(BF16)
            gk_s[...] = t_mm(dscore[:, :own], q_s[rows])
            gv_s[...] = t_mm(probs_b[:, :own], g_s[rows])
        else:
            probs = expo[:, :own] * inv_total
            dscore = (probs * (dprob[:, :own] - delta)).astype(BF16)
            gk_s[...] += t_mm(dscore, q_s[rows])
            gv_s[...] += t_mm(probs.astype(BF16), g_s[rows])
    out_s[...] = (act_s[line : own - line].astype(F32) + mm(attended, wo[...])).astype(BF16)
    for kx, ref in ((0, out0), (1, out1)):
        to_x = x if kx == 0 else 1 - x
        ref[...] = out_s[pl.ds(pl.multiple_of(2 * to_x * line, line), 2 * line)]
    grad_act = cot_s[:own].astype(F32)
    grad_act = grad_act + mm_t(grad_q, wq[...])
    grad_act = grad_act + mm_t((gk_s[...] * scale).astype(BF16), wk[...])
    grad_act = grad_act + mm_t(gv_s[...].astype(BF16), wv[...])
    convf, inverse, normed = norm_parts(conv_s[:own], gain)
    sigma = 1.0 / (1.0 + jnp.exp(-normed))
    scaled = grad_act * sigma * (1.0 + normed * (1.0 - sigma)) * gain
    mean = jnp.mean(scaled * convf, axis=-1, keepdims=True)
    grad_conv = inverse * (scaled - convf * inverse * inverse * mean)
    row = lax.broadcasted_iota(jnp.int32, grad_conv.shape, 0)
    first = jnp.where(q == 0, line, 0)
    last = jnp.where(q == 3, own - line, own)
    inside = jnp.logical_and(row >= first, row < last)
    grad_s[...] = jnp.where(inside, grad_conv, 0.0).astype(BF16)
    for kx, ref in ((0, grad0), (1, grad1)):
        to_x = x if kx == 0 else 1 - x
        ref[...] = grad_s[pl.ds(pl.multiple_of(2 * to_x * line, line), 4 * line)]


def attention(place, convs, cots, gain, wq, wk, wv, wo):
    block, chans = convs[0].shape
    own, whole = 3 * block, 8 * block
    act = lambda n, t=BF16: pltpu.VMEM((n, chans), t)
    return pl.pallas_call(
        attention_kernel,
        in_specs=[SM] + [VM] * (len(convs) + len(cots) + 5),
        out_specs=[VM] * 4,
        out_shape=[jax.ShapeDtypeStruct((n * block, chans), BF16) for n in (1, 1, 2, 2)],
        scratch_shapes=[act(whole), act(whole), act(own)]
        + [act(whole)] * 4
        + [act(own, F32), act(own, F32), act(2 * block), act(own)],
        compiler_params=pltpu.CompilerParams(vmem_limit_bytes=26 * MIB),
        cost_estimate=pl.CostEstimate(
            flops=4 * 10**9, bytes_accessed=4 * 10**6, transcendentals=1 << 20
        ),
        name="attention",
    )(place, *convs, *cots, gain, wq, wk, wv, wo)


def site(h, c, y, x):
    return (h * 2 + c) * 8 + 2 * y + x


def send(value, runs, to):
    pairs = []
    for h in range(runs // 2):
        for c in range(2):
            for y in range(4):
                for x in range(2):
                    there = to(c, y, x)
                    if there is not None:
                        pairs.append((site(h, c, y, x), site(h, *there)))
    return lax.ppermute(value, ("tm", "rows"), pairs)


def home(ky, kx):
    return lambda c, y, x: (y % 2, 2 * ((y // 2 + ky) % 2) + c, x ^ kx)


def swap(c, y, x):
    return 1 - c, y, x


def across(c, y, x):
    return c, y, x ^ 1


def beyond(c, y, x):
    y = y + 1 if x else y - 1
    return (c, y, x ^ 1) if 0 <= y < 4 else None


def local(video, conv_weight, norm_gain, w_query, w_key, w_value, w_out, cotangent):
    frames, height, width, chans = video.shape
    runs, slabs = lax.axis_size("tm"), lax.axis_size("rows")
    assert (frames, height, slabs) == (2, 2, 8)
    slab_at = lax.axis_index("rows")
    x = slab_at % 2
    quarter = 2 * (slab_at // 4) + lax.axis_index("tm") % 2
    place = jnp.stack([x, quarter]).astype(jnp.int32)
    block = 2 * width

    packet, far, cot_same, held = prepare(place, video, cotangent.reshape(2, block, chans))
    far = send(far, runs, beyond)
    packet = send(packet, runs, across)
    weight = load(conv_weight)
    cot_own = join(cot_same, packet)
    cot_b = send(cot_own, runs, home(0, 0))
    slab = (packet, held, far)

    def forward(main, side, src, dst, dtype):
        kernel = functools.partial(forward_kernel, main, side, src, dst)
        return conv_call(kernel, place, slab, weight, width, dtype)

    def backward(main, side, src, dst, dtype):
        kernel = functools.partial(backward_kernel, main, side, src, dst)
        return conv_call(kernel, place, slab, weight, width, dtype)

    for_next = forward(0, 1, 1, 0, BF16)
    cached = lax.ppermute(for_next, "tm", [(i, i + 1) for i in range(runs - 1)])
    own = forward(2, 1, 0, 1, F32)
    cot_c = send(cot_b, runs, lambda c, y, x: (c, y ^ 2, x))
    same, other = merge(place, own, cached)
    got, swapped = {}, {}
    for ky, kx in ((1, 1), (0, 1), (1, 0), (0, 0)):
        got[ky, kx] = send(other if kx else same, runs, home(ky, kx))
    cots = [cot_b, cot_c, send(cot_b, runs, swap), send(cot_c, runs, swap)]
    for ky, kx in ((1, 1), (0, 1), (1, 0), (0, 0)):
        swapped[ky, kx] = send(got[ky, kx], runs, swap)
    order = ((0, 0), (0, 1), (1, 0), (1, 1))
    convs = [got[k] for k in order] + [swapped[k] for k in order]

    out0, out1, grad0, grad1 = attention(
        place, convs, cots, norm_gain.reshape(1, chans), w_query, w_key, w_value, w_out
    )
    grad1 = send(grad1, runs, home(0, 1))
    grad0 = send(grad0, runs, home(0, 0))
    out0 = send(out0, runs, home(0, 0))
    out1 = send(out1, runs, home(0, 1))
    slab = (grad0, grad1)
    for_last = backward(0, 1, 0, 1, BF16)
    handed = lax.ppermute(for_last, "tm", [(i + 1, i) for i in range(runs - 1)])
    own_grad = backward(2, 1, 1, 0, F32)
    block_out, video_grad = finish(place, out0, out1, own_grad, handed)
    return block_out.reshape(video.shape), video_grad.reshape(video.shape)


def solution(mesh):
    spec = P("tm", "rows", None, None)
    return jax.shard_map(
        local,
        mesh=mesh,
        in_specs=(spec, P(), P(), P(), P(), P(), P(), spec),
        out_specs=(spec, spec),
        check_vma=False,
    )
```

```python
import functools

import jax
import jax.numpy as jnp
from jax import lax
from jax.experimental import pallas as pl
from jax.experimental.pallas import tpu as pltpu
from jax.sharding import PartitionSpec as P


F32 = jnp.float32
BF16 = jnp.bfloat16
MIB = 1024 * 1024
LOAD = 42 * MIB
VM = pl.BlockSpec(memory_space=pltpu.VMEM)
SM = pl.BlockSpec(memory_space=pltpu.SMEM)
HBM = pl.BlockSpec(memory_space=pltpu.HBM)


def call(kernel, operands, specs, shapes, scratch, limit, cost=0, outs=VM):
    return pl.pallas_call(
        kernel,
        in_specs=specs,
        out_specs=[outs] * len(shapes),
        out_shape=[jax.ShapeDtypeStruct(dims, dtype) for dims, dtype in shapes],
        scratch_shapes=scratch,
        compiler_params=pltpu.CompilerParams(vmem_limit_bytes=limit),
        cost_estimate=pl.CostEstimate(flops=cost, bytes_accessed=1 << 20, transcendentals=0),
    )(*operands)


def pick_kernel(place, first, second, same, other):
    x = place[0]
    half = first.shape[1]
    for n, ref in enumerate((first, second)):
        same[n * half : (n + 1) * half] = ref[x]
        other[n * half : (n + 1) * half] = ref[1 - x]


def pick(place, first, second):
    shape = (2 * first.shape[1], first.shape[2])
    return call(pick_kernel, (place, first, second), [SM, VM, VM], [(shape, BF16)] * 2, [], 8 * MIB)


def merge_kernel(place, own, cached, same, other):
    x = place[0]
    same[...] = (own[x] + cached[x].astype(F32)).astype(BF16)
    other[...] = (own[1 - x] + cached[1 - x].astype(F32)).astype(BF16)


def merge(place, own, cached):
    return call(
        merge_kernel, (place, own, cached), [SM, VM, VM], [(own.shape[1:], BF16)] * 2, [], 8 * MIB
    )


def load_kernel(w_hbm, w_out, sem):
    copy = pltpu.make_async_copy(w_hbm, w_out, sem)
    copy.start()
    copy.wait()


def load(weight):
    return call(
        load_kernel, (weight,), [HBM], [(weight.shape, BF16)], [pltpu.SemaphoreType.DMA], LOAD
    )[0]


def deliver_kernel(place, out0, out1, block_out, sems):
    x = place[0]
    copies = [
        pltpu.make_async_copy(out0, block_out.at[x], sems.at[0]),
        pltpu.make_async_copy(out1, block_out.at[1 - x], sems.at[1]),
    ]
    for copy in copies:
        copy.start()
    for copy in copies:
        copy.wait()


def deliver(place, out0, out1):
    return call(
        deliver_kernel, (place, out0, out1), [SM, VM, VM], [((2,) + out0.shape, BF16)],
        [pltpu.SemaphoreType.DMA((2,))], 8 * MIB, outs=HBM,
    )[0]


def finish_kernel(own, handed, video_grad, total, sems):
    copies = []
    for f in range(2):
        total[f] = (own[f] + handed[f].astype(F32)).astype(BF16)
        copies.append(pltpu.make_async_copy(total.at[f], video_grad.at[f], sems.at[f]))
        copies[f].start()
    for copy in copies:
        copy.wait()


def finish(own, handed):
    return call(
        finish_kernel, (own, handed), [VM, VM], [(own.shape, BF16)],
        [pltpu.VMEM(own.shape, BF16), pltpu.SemaphoreType.DMA((2,))], 8 * MIB, outs=HBM,
    )[0]


def spread(rows_f32, width):
    n = rows_f32.shape[0]
    col = lax.broadcasted_iota(jnp.int32, rows_f32.shape, 0) % width
    left = jnp.where(col == 0, 0.0, pltpu.roll(rows_f32, 1, 0))
    right = jnp.where(col == width - 1, 0.0, pltpu.roll(rows_f32, n - 1, 0))
    return left, rows_f32, right


def fill(taps, frame, row, block, width, flip):
    n, _, chans = block.shape
    shifted = spread(block.astype(F32).reshape(n * width, chans), width)
    if flip:
        shifted = shifted[::-1]
    for c in range(3):
        taps[frame, row : row + n, :, c * chans : (c + 1) * chans] = (
            shifted[c].astype(BF16).reshape(n, width, chans)
        )


def conv_steps(taps, w_ref, main, side, out, src, dst, transposed):
    chans = w_ref.shape[-1]

    def times(lhs, a, b):
        if not transposed:
            return mm(lhs, w_ref[a, b].reshape(3 * chans, chans))
        return mm_t(lhs, jnp.concatenate([w_ref[a, b, c] for c in range(3)], axis=1))

    both = extra = None
    for b in range(3):
        row = (2 - b) if transposed else b
        lhs = [taps[f, row : row + 2] for f in range(2)]
        lhs = [v.reshape(v.shape[0] * v.shape[1], v.shape[2]) for v in lhs]
        term = times(jnp.concatenate(lhs, axis=0), main, b)
        both = term if both is None else both + term
        term = times(lhs[src], side, b)
        extra = term if extra is None else extra + term
    half = both.shape[0] // 2
    for f in range(2):
        term = both[f * half : (f + 1) * half]
        out[f] = (term + extra if f == dst else term).astype(out.dtype)


def forward_kernel(main, side, src, dst, place, near, mid, far, w_ref, out, taps):
    width = mid.shape[2]
    swapped = place[0] == 1
    for f in range(2):
        fill(taps, f, 0, jnp.where(swapped, near[f], far[f])[None], width, False)
        fill(taps, f, 1, mid[f], width, False)
        fill(taps, f, 3, jnp.where(swapped, far[f], near[f])[None], width, False)
    conv_steps(taps, w_ref, main, side, out, src, dst, False)


def backward_kernel(main, side, src, dst, place, r0, r1, w_ref, out, taps):
    width, chans = taps.shape[2], w_ref.shape[-1]
    swapped = place[0] == 1
    for f, (a, b) in enumerate(((r0, r1), (r1, r0))):
        rows = jnp.where(swapped, b[...], a[...])
        fill(taps, f, 0, rows.reshape(4, width, chans), width, True)
    conv_steps(taps, w_ref, main, side, out, src, dst, True)


def conv_call(kernel, place, operands, weight, width, dtype):
    chans = weight.shape[-1]
    return call(
        kernel, (place, *operands, weight), [SM] + [VM] * (len(operands) + 1),
        [((2, 2 * width, chans), dtype)], [pltpu.VMEM((2, 4, width, 3 * chans), BF16)],
        24 * MIB, 2 * 9 * 3 * 128 * chans * chans,
    )[0]


def norm_parts(conv, gain):
    convf = conv.astype(F32)
    inverse = lax.rsqrt(jnp.mean(convf * convf, axis=-1, keepdims=True) + 1e-06)
    normed = convf * inverse * gain
    return convf, inverse, normed


def mm(a, b):
    return jnp.dot(a, b, preferred_element_type=F32)


def mm_t(a, b):
    return lax.dot_general(a, b, (((1,), (1,)), ((), ())), preferred_element_type=F32)


def t_mm(a, b):
    return lax.dot_general(a, b, (((0,), (0,)), ((), ())), preferred_element_type=F32)


CHUNKS = ((0, 384), (384, 256), (640, 256), (896, 128))


def put(dst, value, place, quarter, kx):
    x, q = place[0], place[1]
    line = value.shape[0] // 2
    for j in range(2):
        slot = (4 * (quarter - q) + 2 * (x + kx - 2 * x * kx) + j + 17) % 16
        dst[pl.ds(pl.multiple_of(slot * line, line), line)] = value[j * line : (j + 1) * line]


def quarters(q):
    side = q + 1 - 2 * (q % 2)
    return q, (q + 2) % 4, side, (side + 2) % 4


def attend_kernel(
    place, c00, c01, c10, c11, s00, s01, s10, s11, gain_ref, wq, wk, wv, wo,
    q_s, k_s, v_s, p_s, conv_own, out0, out1, conv_s, out_s,
):
    x = place[0]
    line = c00.shape[0] // 2
    own = 6 * line
    chans = wq.shape[0]
    scale = 1.0 / jnp.sqrt(jnp.float32(chans))
    gain = gain_ref[...]
    q, far, side, far_side = quarters(place[1])
    for ref, quarter, kx in (
        (c00, q, 0), (c01, q, 1), (c10, far, 0), (c11, far, 1),
        (s00, side, 0), (s01, side, 1), (s10, far_side, 0), (s11, far_side, 1),
    ):
        put(conv_s, ref, place, quarter, kx)
    conv_own[...] = conv_s[:own]

    act_own = None
    for at, n in CHUNKS:
        rows = slice(at, at + n)
        _, _, normed = norm_parts(conv_s[rows], gain)
        act = (normed / (1.0 + jnp.exp(-normed))).astype(BF16)
        if at == 0:
            act_own = act[line : own - line]
        q_s[rows] = mm(act, wq[...]).astype(BF16)
        k_s[rows] = mm(act, wk[...]).astype(BF16)
        v_s[rows] = mm(act, wv[...]).astype(BF16)
    for at, n in CHUNKS:
        rows = slice(at, at + n)
        scores = mm_t(q_s[rows], k_s[...]) * scale
        top = jnp.max(scores, axis=-1, keepdims=True)
        expo = jnp.exp(scores - top)
        probs = (expo * (1.0 / jnp.sum(expo, axis=-1, keepdims=True))).astype(BF16)
        p_s[rows] = probs
        if at == 0:
            attended = mm(probs[line : own - line], v_s[...]).astype(BF16)
            out_s[...] = (act_own.astype(F32) + mm(attended, wo[...])).astype(BF16)
    for kx, ref in ((0, out0), (1, out1)):
        to_x = x if kx == 0 else 1 - x
        ref[...] = out_s[pl.ds(pl.multiple_of(2 * to_x * line, line), 2 * line)]


def attend(place, convs, gain, wq, wk, wv, wo):
    block, chans = convs[0].shape
    own, whole = 3 * block, 8 * block
    return call(
        attend_kernel, (place, *convs, gain, wq, wk, wv, wo), [SM] + [VM] * 13,
        [((whole, chans), BF16)] * 3
        + [((whole, whole), BF16), ((own, chans), BF16)]
        + [((block, chans), BF16)] * 2,
        [pltpu.VMEM((whole, chans), BF16), pltpu.VMEM((2 * block, chans), BF16)],
        26 * MIB, 2 * 10**9,
    )


def attend_grad_kernel(
    place, q_s, k_s, v_s, p_s, conv_own, same, other, same_side, other_side,
    gain_ref, wq, wk, wv, wo,
    grad0, grad1, cot_s, g_s, gk_s, gv_s, grad_s,
):
    x = place[0]
    block = same.shape[0] // 2
    line = block // 2
    own = 6 * line
    chans = wq.shape[0]
    scale = 1.0 / jnp.sqrt(jnp.float32(chans))
    gain = gain_ref[...]
    q, far, side, far_side = quarters(place[1])
    for kx, near_ref, side_ref in ((0, same, same_side), (1, other, other_side)):
        for n in range(2):
            half = slice(n * block, (n + 1) * block)
            put(cot_s, near_ref.at[half], place, (q, far)[n], kx)
            put(cot_s, side_ref.at[half], place, (side, far_side)[n], kx)

    grad_q = None
    for at, n in CHUNKS:
        rows = slice(at, at + n)
        g_s[rows] = mm_t(cot_s[rows], wo[...]).astype(BF16)
        dprob = mm_t(g_s[rows], v_s[...])
        if at == 0:
            probs = p_s[rows].astype(F32)
            delta = jnp.sum(probs * dprob, axis=-1, keepdims=True)
            dscore = (probs * (dprob - delta)).astype(BF16)
            grad_q = (mm(dscore, k_s[...]) * scale).astype(BF16)
            gk_s[...] = t_mm(dscore[:, :own], q_s[rows])
            gv_s[...] = t_mm(p_s[rows, :own], g_s[rows])
        else:
            delta = jnp.sum(p_s[rows].astype(F32) * dprob, axis=-1, keepdims=True)
            dscore = (p_s[rows, :own].astype(F32) * (dprob[:, :own] - delta)).astype(BF16)
            gk_s[...] += t_mm(dscore, q_s[rows])
            gv_s[...] += t_mm(p_s[rows, :own], g_s[rows])
    grad_act = cot_s[:own].astype(F32)
    grad_act = grad_act + mm_t(grad_q, wq[...])
    grad_act = grad_act + mm_t((gk_s[...] * scale).astype(BF16), wk[...])
    grad_act = grad_act + mm_t(gv_s[...].astype(BF16), wv[...])
    convf, inverse, normed = norm_parts(conv_own[...], gain)
    sigma = 1.0 / (1.0 + jnp.exp(-normed))
    scaled = grad_act * sigma * (1.0 + normed * (1.0 - sigma)) * gain
    mean = jnp.mean(scaled * convf, axis=-1, keepdims=True)
    grad_conv = inverse * (scaled - convf * inverse * inverse * mean)
    row = lax.broadcasted_iota(jnp.int32, grad_conv.shape, 0)
    first = jnp.where(q == 0, line, 0)
    last = jnp.where(q == 3, own - line, own)
    inside = jnp.logical_and(row >= first, row < last)
    grad_s[...] = jnp.where(inside, grad_conv, 0.0).astype(BF16)
    for kx, ref in ((0, grad0), (1, grad1)):
        to_x = x if kx == 0 else 1 - x
        ref[...] = grad_s[pl.ds(pl.multiple_of(2 * to_x * line, line), 4 * line)]


def attend_grad(place, saved, cots, gain, wq, wk, wv, wo):
    own, chans = saved[-1].shape
    whole = saved[0].shape[0]
    act = lambda n, t=BF16: pltpu.VMEM((n, chans), t)
    return call(
        attend_grad_kernel, (place, *saved, *cots, gain, wq, wk, wv, wo), [SM] + [VM] * 14,
        [((2 * own // 3, chans), BF16)] * 2,
        [act(whole), act(whole), act(own, F32), act(own, F32), act(own)],
        26 * MIB, 2 * 10**9,
    )


def site(h, c, y, x):
    return (h * 2 + c) * 8 + 2 * y + x


def send(value, runs, to):
    pairs = []
    for h in range(runs // 2):
        for c in range(2):
            for y in range(4):
                for x in range(2):
                    there = to(c, y, x)
                    if there is not None:
                        pairs.append((site(h, c, y, x), site(h, *there)))
    return lax.ppermute(value, ("tm", "rows"), pairs)


def home(ky, kx):
    return lambda c, y, x: (y % 2, 2 * ((y // 2 + ky) % 2) + c, x ^ kx)


def swap(c, y, x):
    return 1 - c, y, x


def across(c, y, x):
    return c, y, x ^ 1


def beyond(c, y, x):
    y = y + 1 if x else y - 1
    return (c, y, x ^ 1) if 0 <= y < 4 else None


def local(video, conv_weight, norm_gain, w_query, w_key, w_value, w_out, cotangent):
    frames, height, width, chans = video.shape
    runs, slabs = lax.axis_size("tm"), lax.axis_size("rows")
    assert (frames, height, slabs) == (2, 2, 8)
    slab_at = lax.axis_index("rows")
    x = slab_at % 2
    quarter = 2 * (slab_at // 4) + lax.axis_index("tm") % 2
    place = jnp.stack([x, quarter]).astype(jnp.int32)
    block = 2 * width

    cot_b = send(cotangent.reshape(2, block, chans), runs, home(0, 0))
    far = send(lax.dynamic_index_in_dim(video, x, 1, keepdims=False), runs, beyond)
    near = send(lax.dynamic_index_in_dim(video, 1 - x, 1, keepdims=False), runs, across)
    weight = load(conv_weight)
    slab = (near, video, far)

    def forward(main, side, src, dst, dtype):
        kernel = functools.partial(forward_kernel, main, side, src, dst)
        return conv_call(kernel, place, slab, weight, width, dtype)

    def backward(main, side, src, dst, dtype):
        kernel = functools.partial(backward_kernel, main, side, src, dst)
        return conv_call(kernel, place, slab, weight, width, dtype)

    for_next = forward(0, 1, 1, 0, BF16)
    cached = lax.ppermute(for_next, "tm", [(i, i + 1) for i in range(runs - 1)])
    own = forward(2, 1, 0, 1, F32)
    cot_c = send(cot_b, runs, lambda c, y, x: (c, y ^ 2, x))
    cot_same, cot_other = pick(place, cot_b, cot_c)
    same, other = merge(place, own, cached)
    got, swapped = {}, {}
    for ky, kx in ((1, 1), (0, 1), (1, 0), (0, 0)):
        got[ky, kx] = send(other if kx else same, runs, home(ky, kx))
    for ky, kx in ((1, 1), (0, 1), (1, 0), (0, 0)):
        swapped[ky, kx] = send(got[ky, kx], runs, swap)
    order = ((0, 0), (0, 1), (1, 0), (1, 1))
    convs = [got[k] for k in order] + [swapped[k] for k in order]

    cot_other = send(cot_other, runs, across)
    projections = (norm_gain.reshape(1, chans), w_query, w_key, w_value, w_out)
    *saved, out0, out1 = attend(place, convs, *projections)
    cots = (
        cot_same, cot_other,
        send(cot_same, runs, swap), send(cot_other, runs, swap),
    )
    out1 = send(out1, runs, home(0, 1))
    out0 = send(out0, runs, home(0, 0))
    grad0, grad1 = attend_grad(place, saved, cots, *projections)
    grad1 = send(grad1, runs, home(0, 1))
    grad0 = send(grad0, runs, home(0, 0))
    slab = (grad0, grad1)
    for_last = backward(0, 1, 0, 1, BF16)
    handed = lax.ppermute(for_last, "tm", [(i + 1, i) for i in range(runs - 1)])
    own_grad = backward(2, 1, 1, 0, F32)
    block_out = deliver(place, out0, out1)
    video_grad = finish(own_grad, handed)
    return block_out.reshape(video.shape), video_grad.reshape(video.shape)


def solution(mesh):
    spec = P("tm", "rows", None, None)
    return jax.shard_map(
        local,
        mesh=mesh,
        in_specs=(spec, P(), P(), P(), P(), P(), P(), spec),
        out_specs=(spec, spec),
        check_vma=False,
    )
```

```python
import functools

import jax
import jax.numpy as jnp
from jax import lax
from jax.experimental import pallas as pl
from jax.experimental.pallas import tpu as pltpu
from jax.sharding import PartitionSpec as P


F32 = jnp.float32
BF16 = jnp.bfloat16
MIB = 1024 * 1024
LOAD = 42 * MIB
VM = pl.BlockSpec(memory_space=pltpu.VMEM)
SM = pl.BlockSpec(memory_space=pltpu.SMEM)
HBM = pl.BlockSpec(memory_space=pltpu.HBM)


def call(kernel, operands, specs, shapes, scratch, limit, cost=0, outs=VM):
    return pl.pallas_call(
        kernel,
        in_specs=specs,
        out_specs=[outs] * len(shapes),
        out_shape=[jax.ShapeDtypeStruct(dims, dtype) for dims, dtype in shapes],
        scratch_shapes=scratch,
        compiler_params=pltpu.CompilerParams(vmem_limit_bytes=limit),
        cost_estimate=pl.CostEstimate(flops=cost, bytes_accessed=1 << 20, transcendentals=0),
    )(*operands)


def pick_kernel(place, both, same, other):
    x = place[0]
    same[...] = both[x]
    other[...] = both[1 - x]


def pick(place, both):
    return call(
        pick_kernel, (place, both), [SM, VM], [(both.shape[1:], both.dtype)] * 2, [], 4 * MIB
    )


def join_kernel(place, same, other, out):
    x = place[0]
    half = same.shape[0]
    out[pl.ds(pl.multiple_of(x * half, half), half)] = same[...]
    out[pl.ds(pl.multiple_of((1 - x) * half, half), half)] = other[...]


def join(place, same, other):
    shape = (2 * same.shape[0], same.shape[1])
    return call(join_kernel, (place, same, other), [SM, VM, VM], [(shape, BF16)], [], 4 * MIB)[0]


def merge_kernel(own, cached, out):
    out[...] = (own[...] + cached[...].astype(F32)).astype(BF16)


def merge(own, cached):
    return call(merge_kernel, (own, cached), [VM, VM], [(own.shape, BF16)], [], 8 * MIB)[0]


def load_kernel(w_hbm, w_out, sem):
    copy = pltpu.make_async_copy(w_hbm, w_out, sem)
    copy.start()
    copy.wait()


def load(weight):
    return call(
        load_kernel, (weight,), [HBM], [(weight.shape, BF16)], [pltpu.SemaphoreType.DMA], LOAD
    )[0]


def deliver_kernel(place, out0, out1, block_out, sems):
    x = place[0]
    copies = [
        pltpu.make_async_copy(out0, block_out.at[x], sems.at[0]),
        pltpu.make_async_copy(out1, block_out.at[1 - x], sems.at[1]),
    ]
    for copy in copies:
        copy.start()
    for copy in copies:
        copy.wait()


def deliver(place, out0, out1):
    return call(
        deliver_kernel, (place, out0, out1), [SM, VM, VM], [((2,) + out0.shape, BF16)],
        [pltpu.SemaphoreType.DMA((2,))], 8 * MIB, outs=HBM,
    )[0]


def finish_kernel(own, handed, video_grad, total, sems):
    copies = []
    for f in range(2):
        total[f] = (own[f] + handed[f].astype(F32)).astype(BF16)
        copies.append(pltpu.make_async_copy(total.at[f], video_grad.at[f], sems.at[f]))
        copies[f].start()
    for copy in copies:
        copy.wait()


def finish(own, handed):
    return call(
        finish_kernel, (own, handed), [VM, VM], [(own.shape, BF16)],
        [pltpu.VMEM(own.shape, BF16), pltpu.SemaphoreType.DMA((2,))], 8 * MIB, outs=HBM,
    )[0]


def spread(rows_f32, width):
    n = rows_f32.shape[0]
    col = lax.broadcasted_iota(jnp.int32, rows_f32.shape, 0) % width
    left = jnp.where(col == 0, 0.0, pltpu.roll(rows_f32, 1, 0))
    right = jnp.where(col == width - 1, 0.0, pltpu.roll(rows_f32, n - 1, 0))
    return left, rows_f32, right


def fill(taps, frame, row, block, width, flip):
    n, _, chans = block.shape
    shifted = spread(block.astype(F32).reshape(n * width, chans), width)
    if flip:
        shifted = shifted[::-1]
    for c in range(3):
        taps[frame, row : row + n, :, c * chans : (c + 1) * chans] = (
            shifted[c].astype(BF16).reshape(n, width, chans)
        )


def conv_steps(taps, w_ref, main, side, out, src, dst, transposed):
    chans = w_ref.shape[-1]

    def times(lhs, a, b):
        if not transposed:
            return mm(lhs, w_ref[a, b].reshape(3 * chans, chans))
        return mm_t(lhs, jnp.concatenate([w_ref[a, b, c] for c in range(3)], axis=1))

    both = extra = None
    for b in range(3):
        row = (2 - b) if transposed else b
        lhs = [taps[f, row : row + 2] for f in range(2)]
        lhs = [v.reshape(v.shape[0] * v.shape[1], v.shape[2]) for v in lhs]
        term = times(jnp.concatenate(lhs, axis=0), main, b)
        both = term if both is None else both + term
        term = times(lhs[src], side, b)
        extra = term if extra is None else extra + term
    half = both.shape[0] // 2
    for f in range(2):
        term = both[f * half : (f + 1) * half]
        out[f] = (term + extra if f == dst else term).astype(out.dtype)


def frame_taps(taps, frame, rows):
    piece = taps[frame, rows : rows + 4]
    return piece.reshape(piece.shape[0] * piece.shape[1], piece.shape[2])


def frame_conv(taps, w_ref, frame, a):
    chans = w_ref.shape[-1]
    total = None
    for b in range(3):
        term = mm(frame_taps(taps, frame, b), w_ref[a, b].reshape(3 * chans, chans))
        total = term if total is None else total + term
    return total


def next_kernel(place, mine, packet, far_same, far_other, w_ref, out, taps, acc):
    x = place[0]
    flip = x == 1
    width = taps.shape[2]
    chans = w_ref.shape[-1]
    for f in range(2):
        line = slice(f * width, (f + 1) * width)
        pair = slice(2 * f * width, 2 * (f + 1) * width)
        a, b = mine[pair], packet[pair]
        top = jnp.where(flip, far_same[line], far_other[line])
        bottom = jnp.where(flip, far_other[line], far_same[line])
        for row, rows in (
            (0, top), (1, jnp.where(flip, b, a)), (3, jnp.where(flip, a, b)), (5, bottom)
        ):
            fill(taps, f, row, rows.reshape(-1, width, chans), width, False)
    acc[...] = frame_conv(taps, w_ref, x, 0)

    @pl.when(x == 0)
    def _():
        acc[...] += frame_conv(taps, w_ref, 1, 1)

    out[...] = acc[...].astype(out.dtype)


def own_kernel(place, taps, w_ref, out):
    x = place[0]
    out[...] = frame_conv(taps, w_ref, x, 2)

    @pl.when(x == 1)
    def _():
        out[...] += frame_conv(taps, w_ref, 0, 1)


def backward_kernel(main, side, src, dst, place, r0, r1, w_ref, out, taps):
    width, chans = taps.shape[2], w_ref.shape[-1]
    swapped = place[0] == 1
    for f, (a, b) in enumerate(((r0, r1), (r1, r0))):
        rows = jnp.where(swapped, b[...], a[...])
        fill(taps, f, 0, rows.reshape(4, width, chans), width, True)
    conv_steps(taps, w_ref, main, side, out, src, dst, True)


def conv_call(kernel, place, operands, weight, width, dtype):
    chans = weight.shape[-1]
    return call(
        kernel, (place, *operands, weight), [SM] + [VM] * (len(operands) + 1),
        [((2, 2 * width, chans), dtype)], [pltpu.VMEM((2, 4, width, 3 * chans), BF16)],
        24 * MIB, 2 * 9 * 3 * 128 * chans * chans,
    )[0]


def norm_parts(conv, gain):
    convf = conv.astype(F32)
    inverse = lax.rsqrt(jnp.mean(convf * convf, axis=-1, keepdims=True) + 1e-06)
    normed = convf * inverse * gain
    return convf, inverse, normed


def mm(a, b):
    return jnp.dot(a, b, preferred_element_type=F32)


def mm_t(a, b):
    return lax.dot_general(a, b, (((1,), (1,)), ((), ())), preferred_element_type=F32)


def t_mm(a, b):
    return lax.dot_general(a, b, (((0,), (0,)), ((), ())), preferred_element_type=F32)


CHUNKS = ((0, 384), (384, 256), (640, 256), (896, 128))


def attention_kernel(
    place, c0, c2, c1, c3, t0, t2, t1, t3, gain_ref, wq, wk, wv, wo,
    out0, out1, grad0, grad1, conv_s, cot_s, act_s, q_s, k_s, v_s, g_s, gk_s, gv_s, out_s, grad_s,
):
    x, q = place[0], place[1]
    line = c0.shape[0] // 4
    own = 6 * line
    chans = wq.shape[0]
    scale = 1.0 / jnp.sqrt(jnp.float32(chans))
    gain = gain_ref[...]
    side = q + 1 - 2 * (q % 2)
    quarters = (q, (q + 2) % 4, side, (side + 2) % 4)
    for dst, refs in ((conv_s, (c0, c2, c1, c3)), (cot_s, (t0, t2, t1, t3))):
        for ref, quarter in zip(refs, quarters):
            for j in range(4):
                slot = (4 * (quarter - q) + j + 17) % 16
                dst[pl.ds(pl.multiple_of(slot * line, line), line)] = ref[j * line : (j + 1) * line]

    for at, n in CHUNKS:
        rows = slice(at, at + n)
        _, _, normed = norm_parts(conv_s[rows], gain)
        act = (normed / (1.0 + jnp.exp(-normed))).astype(BF16)
        if at == 0:
            act_s[...] = act
        q_s[rows] = mm(act, wq[...]).astype(BF16)
        k_s[rows] = mm(act, wk[...]).astype(BF16)
        v_s[rows] = mm(act, wv[...]).astype(BF16)
        g_s[rows] = mm_t(cot_s[rows], wo[...]).astype(BF16)
    attended = grad_q = None
    for at, n in CHUNKS:
        rows = slice(at, at + n)
        scores = mm_t(q_s[rows], k_s[...]) * scale
        top = jnp.max(scores, axis=-1, keepdims=True)
        expo = jnp.exp(scores - top)
        inv_total = 1.0 / jnp.sum(expo, axis=-1, keepdims=True)
        dprob = mm_t(g_s[rows], v_s[...])
        delta = jnp.sum(expo * dprob, axis=-1, keepdims=True) * inv_total
        if at == 0:
            probs = expo * inv_total
            probs_b = probs.astype(BF16)
            mid = slice(line, own - line)
            attended = mm(probs_b[mid], v_s[...]).astype(BF16)
            dscore = (probs * (dprob - delta)).astype(BF16)
            grad_q = (mm(dscore, k_s[...]) * scale).astype(BF16)
            gk_s[...] = t_mm(dscore[:, :own], q_s[rows])
            gv_s[...] = t_mm(probs_b[:, :own], g_s[rows])
        else:
            probs = expo[:, :own] * inv_total
            dscore = (probs * (dprob[:, :own] - delta)).astype(BF16)
            gk_s[...] += t_mm(dscore, q_s[rows])
            gv_s[...] += t_mm(probs.astype(BF16), g_s[rows])
    out_s[...] = (act_s[line : own - line].astype(F32) + mm(attended, wo[...])).astype(BF16)
    for kx, ref in ((0, out0), (1, out1)):
        to_x = x if kx == 0 else 1 - x
        ref[...] = out_s[pl.ds(pl.multiple_of(2 * to_x * line, line), 2 * line)]
    grad_act = cot_s[:own].astype(F32)
    grad_act = grad_act + mm_t(grad_q, wq[...])
    grad_act = grad_act + mm_t((gk_s[...] * scale).astype(BF16), wk[...])
    grad_act = grad_act + mm_t(gv_s[...].astype(BF16), wv[...])
    convf, inverse, normed = norm_parts(conv_s[:own], gain)
    sigma = 1.0 / (1.0 + jnp.exp(-normed))
    scaled = grad_act * sigma * (1.0 + normed * (1.0 - sigma)) * gain
    mean = jnp.mean(scaled * convf, axis=-1, keepdims=True)
    grad_conv = inverse * (scaled - convf * inverse * inverse * mean)
    row = lax.broadcasted_iota(jnp.int32, grad_conv.shape, 0)
    first = jnp.where(q == 0, line, 0)
    last = jnp.where(q == 3, own - line, own)
    inside = jnp.logical_and(row >= first, row < last)
    grad_s[...] = jnp.where(inside, grad_conv, 0.0).astype(BF16)
    for kx, ref in ((0, grad0), (1, grad1)):
        to_x = x if kx == 0 else 1 - x
        ref[...] = grad_s[pl.ds(pl.multiple_of(2 * to_x * line, line), 4 * line)]


def attention(place, convs, cots, gain, wq, wk, wv, wo):
    block, chans = convs[0].shape[0] // 2, convs[0].shape[1]
    own, whole = 3 * block, 8 * block
    act = lambda n, t=BF16: pltpu.VMEM((n, chans), t)
    return pl.pallas_call(
        attention_kernel,
        in_specs=[SM] + [VM] * (len(convs) + len(cots) + 5),
        out_specs=[VM] * 4,
        out_shape=[jax.ShapeDtypeStruct((n * block, chans), BF16) for n in (1, 1, 2, 2)],
        scratch_shapes=[act(whole), act(whole), act(own)]
        + [act(whole)] * 4
        + [act(own, F32), act(own, F32), act(2 * block), act(own)],
        compiler_params=pltpu.CompilerParams(vmem_limit_bytes=26 * MIB),
        cost_estimate=pl.CostEstimate(
            flops=4 * 10**9, bytes_accessed=4 * 10**6, transcendentals=1 << 20
        ),
        name="attention",
    )(place, *convs, *cots, gain, wq, wk, wv, wo)


def site(h, c, y, x):
    return (h * 2 + c) * 8 + 2 * y + x


def send(value, runs, to):
    pairs = []
    for h in range(runs // 2):
        for c in range(2):
            for y in range(4):
                for x in range(2):
                    there = to(c, y, x)
                    if there is not None:
                        pairs.append((site(h, c, y, x), site(h, *there)))
    return lax.ppermute(value, ("tm", "rows"), pairs)


def home(ky, kx):
    return lambda c, y, x: (y % 2, 2 * ((y // 2 + ky) % 2) + c, x ^ kx)


def swap(c, y, x):
    return 1 - c, y, x


def across(c, y, x):
    return c, y, x ^ 1


def beyond(c, y, x):
    y = y + 1 if x else y - 1
    return (c, y, x ^ 1) if 0 <= y < 4 else None


def straight(c, y, x):
    y = y + 1 if x else y - 1
    return (c, y, x) if 0 <= y < 4 else None


def local(video, conv_weight, norm_gain, w_query, w_key, w_value, w_out, cotangent):
    frames, height, width, chans = video.shape
    runs, slabs = lax.axis_size("tm"), lax.axis_size("rows")
    assert (frames, height, slabs) == (2, 2, 8)
    slab_at = lax.axis_index("rows")
    x = slab_at % 2
    quarter = 2 * (slab_at // 4) + lax.axis_index("tm") % 2
    place = jnp.stack([x, quarter]).astype(jnp.int32)
    block = 2 * width

    edge = lax.dynamic_index_in_dim(video, x, 1, keepdims=False).reshape(block, chans)
    mine = video.reshape(2 * block, chans)
    far_other = send(edge, runs, beyond)
    packet = send(mine, runs, across)
    far_same = send(edge, runs, straight)
    cot_b = send(cotangent.reshape(2, block, chans), runs, home(0, 0))
    weight = load(conv_weight)
    cot_same, cot_other = pick(place, cot_b)
    quad = (2 * block, chans)
    for_next, taps = call(
        next_kernel, (place, mine, packet, far_same, far_other, weight), [SM] + [VM] * 5,
        [(quad, BF16), ((2, 6, width, 3 * chans), BF16)], [pltpu.VMEM(quad, F32)],
        24 * MIB, 10**9,
    )
    cached = lax.ppermute(for_next, "tm", [(i, i + 1) for i in range(runs - 1)])
    cot_other = send(cot_other, runs, across)
    own = call(
        own_kernel, (place, taps, weight), [SM, VM, VM], [(quad, F32)], [],
        24 * MIB, 10**9,
    )[0]
    cot_b = join(place, cot_same, cot_other)
    cot_c = send(cot_b, runs, lambda c, y, x: (c, y ^ 2, x))
    conv = merge(own, cached)
    conv_c = send(conv, runs, home(1, 0))
    conv_b = send(conv, runs, home(0, 0))
    cots = (cot_b, cot_c, send(cot_b, runs, swap), send(cot_c, runs, swap))
    convs = (conv_b, conv_c, send(conv_b, runs, swap), send(conv_c, runs, swap))
    out0, out1, grad0, grad1 = attention(
        place, convs, cots, norm_gain.reshape(1, chans), w_query, w_key, w_value, w_out
    )
    grad1 = send(grad1, runs, home(0, 1))
    grad0 = send(grad0, runs, home(0, 0))
    out1 = send(out1, runs, home(0, 1))
    out0 = send(out0, runs, home(0, 0))

    def backward(main, side, src, dst, dtype):
        kernel = functools.partial(backward_kernel, main, side, src, dst)
        return conv_call(kernel, place, slab, weight, width, dtype)

    slab = (grad0, grad1)
    for_last = backward(0, 1, 0, 1, BF16)
    handed = lax.ppermute(for_last, "tm", [(i + 1, i) for i in range(runs - 1)])
    own_grad = backward(2, 1, 1, 0, F32)
    block_out = deliver(place, out0, out1)
    video_grad = finish(own_grad, handed)
    return block_out.reshape(video.shape), video_grad.reshape(video.shape)


def solution(mesh):
    spec = P("tm", "rows", None, None)
    return jax.shard_map(
        local,
        mesh=mesh,
        in_specs=(spec, P(), P(), P(), P(), P(), P(), spec),
        out_specs=(spec, spec),
        check_vma=False,
    )
```

```python
import functools

import jax
import jax.numpy as jnp
from jax import lax
from jax.experimental import pallas as pl
from jax.experimental.pallas import tpu as pltpu
from jax.sharding import PartitionSpec as P


F32 = jnp.float32
BF16 = jnp.bfloat16
MIB = 1024 * 1024
LOG2E = 1.4426950408889634
LOAD = 42 * MIB
VM = pl.BlockSpec(memory_space=pltpu.VMEM)
SM = pl.BlockSpec(memory_space=pltpu.SMEM)
HBM = pl.BlockSpec(memory_space=pltpu.HBM)


def call(kernel, operands, specs, shapes, scratch, limit, cost=0, outs=VM):
    return pl.pallas_call(
        kernel,
        in_specs=specs,
        out_specs=list(outs) if isinstance(outs, tuple) else [outs] * len(shapes),
        out_shape=[jax.ShapeDtypeStruct(dims, dtype) for dims, dtype in shapes],
        scratch_shapes=scratch,
        compiler_params=pltpu.CompilerParams(vmem_limit_bytes=limit),
        cost_estimate=pl.CostEstimate(flops=cost, bytes_accessed=1 << 20, transcendentals=0),
    )(*operands)


def join_kernel(place, same, other, out):
    x = place[0]
    half = same.shape[0]
    out[pl.ds(pl.multiple_of(x * half, half), half)] = same[...]
    out[pl.ds(pl.multiple_of((1 - x) * half, half), half)] = other[...]


def join(place, same, other):
    shape = (2 * same.shape[0], same.shape[1])
    return call(join_kernel, (place, same, other), [SM, VM, VM], [(shape, BF16)], [], 4 * MIB)[0]


def load_kernel(w_hbm, w_out, sem):
    copy = pltpu.make_async_copy(w_hbm, w_out, sem)
    copy.start()
    copy.wait()


def load(weight):
    return call(
        load_kernel, (weight,), [HBM], [(weight.shape, BF16)], [pltpu.SemaphoreType.DMA], LOAD
    )[0]


def finish_kernel(own, handed, video_grad, total, sems):
    copies = []
    for f in range(2):
        total[f] = (own[f] + handed[f].astype(F32)).astype(BF16)
        copies.append(pltpu.make_async_copy(total.at[f], video_grad.at[f], sems.at[f]))
        copies[f].start()
    for copy in copies:
        copy.wait()


def finish(own, handed):
    return call(
        finish_kernel, (own, handed), [VM, VM], [(own.shape, BF16)],
        [pltpu.VMEM(own.shape, BF16), pltpu.SemaphoreType.DMA((2,))], 8 * MIB, outs=HBM,
    )[0]


def spread(rows_f32, width):
    n = rows_f32.shape[0]
    col = lax.broadcasted_iota(jnp.int32, rows_f32.shape, 0) % width
    left = jnp.where(col == 0, 0.0, pltpu.roll(rows_f32, 1, 0))
    right = jnp.where(col == width - 1, 0.0, pltpu.roll(rows_f32, n - 1, 0))
    return left, rows_f32, right


def fill(taps, frame, row, block, width, flip):
    n, _, chans = block.shape
    shifted = spread(block.astype(F32).reshape(n * width, chans), width)
    if flip:
        shifted = shifted[::-1]
    for c in range(3):
        taps[frame, row : row + n, :, c * chans : (c + 1) * chans] = (
            shifted[c].astype(BF16).reshape(n, width, chans)
        )


def conv_steps(taps, w_ref, main, side, out, src, dst, transposed):
    chans = w_ref.shape[-1]

    def times(lhs, a, b):
        if not transposed:
            return mm(lhs, w_ref[a, b].reshape(3 * chans, chans))
        return mm_t(lhs, jnp.concatenate([w_ref[a, b, c] for c in range(3)], axis=1))

    both = extra = None
    for b in range(3):
        row = (2 - b) if transposed else b
        lhs = [taps[f, row : row + 2] for f in range(2)]
        lhs = [v.reshape(v.shape[0] * v.shape[1], v.shape[2]) for v in lhs]
        term = times(jnp.concatenate(lhs, axis=0), main, b)
        both = term if both is None else both + term
        term = times(lhs[src], side, b)
        extra = term if extra is None else extra + term
    half = both.shape[0] // 2
    for f in range(2):
        term = both[f * half : (f + 1) * half]
        out[f] = (term + extra if f == dst else term).astype(out.dtype)


def frame_taps(taps, frame, rows):
    piece = taps[frame, rows : rows + 4]
    return piece.reshape(piece.shape[0] * piece.shape[1], piece.shape[2])


def frame_conv(taps, w_ref, frame, a):
    chans = w_ref.shape[-1]
    total = None
    for b in range(3):
        term = mm(frame_taps(taps, frame, b), w_ref[a, b].reshape(3 * chans, chans))
        total = term if total is None else total + term
    return total


def next_kernel(place, mine, packet, far_same, far_other, w_ref, out, taps, acc):
    x = place[0]
    flip = x == 1
    width = taps.shape[2]
    chans = w_ref.shape[-1]
    for f in range(2):
        line = slice(f * width, (f + 1) * width)
        pair = slice(2 * f * width, 2 * (f + 1) * width)
        a, b = mine[pair], packet[pair]
        top = jnp.where(flip, far_same[line], far_other[line])
        bottom = jnp.where(flip, far_other[line], far_same[line])
        for row, rows in (
            (0, top), (1, jnp.where(flip, b, a)), (3, jnp.where(flip, a, b)), (5, bottom)
        ):
            fill(taps, f, row, rows.reshape(-1, width, chans), width, False)
    acc[...] = frame_conv(taps, w_ref, x, 0)

    @pl.when(x == 0)
    def _():
        acc[...] += frame_conv(taps, w_ref, 1, 1)

    out[...] = acc[...].astype(out.dtype)


def own_kernel(place, taps, w_ref, out):
    x = place[0]
    out[...] = frame_conv(taps, w_ref, x, 2)

    @pl.when(x == 1)
    def _():
        out[...] += frame_conv(taps, w_ref, 0, 1)


def backward_kernel(main, side, src, dst, place, r0, r1, w_ref, out, taps):
    width, chans = taps.shape[2], w_ref.shape[-1]
    swapped = place[0] == 1
    for f, (a, b) in enumerate(((r0, r1), (r1, r0))):
        rows = jnp.where(swapped, b[...], a[...])
        fill(taps, f, 0, rows.reshape(4, width, chans), width, True)
    conv_steps(taps, w_ref, main, side, out, src, dst, True)


def last_kernel(place, r0, r1, out0, out1, w_ref, out, block_out, taps, sems):
    x = place[0]
    copies = [
        pltpu.make_async_copy(out0, block_out.at[x], sems.at[0]),
        pltpu.make_async_copy(out1, block_out.at[1 - x], sems.at[1]),
    ]
    for copy in copies:
        copy.start()
    backward_kernel(2, 1, 1, 0, place, r0, r1, w_ref, out, taps)
    for copy in copies:
        copy.wait()


def conv_call(kernel, place, operands, weight, width, dtype):
    chans = weight.shape[-1]
    return call(
        kernel, (place, *operands, weight), [SM] + [VM] * (len(operands) + 1),
        [((2, 2 * width, chans), dtype)], [pltpu.VMEM((2, 4, width, 3 * chans), BF16)],
        24 * MIB, 2 * 9 * 3 * 128 * chans * chans,
    )[0]


def norm_parts(conv, gain):
    convf = conv.astype(F32)
    inverse = lax.rsqrt(jnp.mean(convf * convf, axis=-1, keepdims=True) + 1e-06)
    normed = convf * inverse * gain
    return convf, inverse, normed


def mm(a, b):
    return jnp.dot(a, b, preferred_element_type=F32)


def mm_t(a, b):
    return lax.dot_general(a, b, (((1,), (1,)), ((), ())), preferred_element_type=F32)


def t_mm(a, b):
    return lax.dot_general(a, b, (((0,), (0,)), ((), ())), preferred_element_type=F32)


CHUNKS = ((0, 384), (384, 256), (640, 256), (896, 128))


def attention_kernel(
    place, c0, c2, c1, c3, t0, t2, t1, t3, gain_ref, wq, wk, wv, wo,
    out0, out1, grad0, grad1, conv_s, cot_s, act_s, q_s, k_s, v_s, g_s, gk_s, gv_s, out_s, grad_s,
):
    x, q = place[0], place[1]
    line = c0.shape[0] // 4
    own = 6 * line
    chans = wq.shape[0]
    scale = 1.0 / jnp.sqrt(jnp.float32(chans))
    gain = gain_ref[...]
    side = q + 1 - 2 * (q % 2)
    quarters = (q, (q + 2) % 4, side, (side + 2) % 4)
    for dst, refs in ((conv_s, (c0, c2, c1, c3)), (cot_s, (t0, t2, t1, t3))):
        for ref, quarter in zip(refs, quarters):
            for j in range(4):
                slot = (4 * (quarter - q) + j + 17) % 16
                dst[pl.ds(pl.multiple_of(slot * line, line), line)] = ref[j * line : (j + 1) * line]

    for at, n in CHUNKS:
        rows = slice(at, at + n)
        _, _, normed = norm_parts(conv_s[rows], gain)
        act = (normed / (1.0 + jnp.exp(-normed))).astype(BF16)
        if at == 0:
            act_s[...] = act
        q_s[rows] = mm(act, wq[...]).astype(BF16)
        k_s[rows] = mm(act, wk[...]).astype(BF16)
        v_s[rows] = mm(act, wv[...]).astype(BF16)
        g_s[rows] = mm_t(cot_s[rows], wo[...]).astype(BF16)
    attended = grad_q = None

    def products(at, n):
        rows = slice(at, at + n)
        return mm_t(q_s[rows], k_s[...]), mm_t(g_s[rows], v_s[...])

    ahead = products(*CHUNKS[0])
    for i, (at, n) in enumerate(CHUNKS):
        rows = slice(at, at + n)
        scores, dprob = ahead
        if i + 1 < len(CHUNKS):
            ahead = products(*CHUNKS[i + 1])
        top = jnp.max(scores, axis=-1, keepdims=True)
        expo = jnp.exp2((scores - top) * (scale * LOG2E))
        inv_total = 1.0 / jnp.sum(expo, axis=-1, keepdims=True)
        delta = jnp.sum(expo * dprob, axis=-1, keepdims=True) * inv_total
        if at == 0:
            probs = expo * inv_total
            probs_b = probs.astype(BF16)
            mid = slice(line, own - line)
            attended = mm(probs_b[mid], v_s[...]).astype(BF16)
            dscore = (probs * (dprob - delta)).astype(BF16)
            grad_q = (mm(dscore, k_s[...]) * scale).astype(BF16)
            gk_s[...] = t_mm(dscore[:, :own], q_s[rows])
            gv_s[...] = t_mm(probs_b[:, :own], g_s[rows])
        else:
            probs = expo[:, :own] * inv_total
            dscore = (probs * (dprob[:, :own] - delta)).astype(BF16)
            gk_s[...] += t_mm(dscore, q_s[rows])
            gv_s[...] += t_mm(probs.astype(BF16), g_s[rows])
    out_s[...] = (act_s[line : own - line].astype(F32) + mm(attended, wo[...])).astype(BF16)
    for kx, ref in ((0, out0), (1, out1)):
        to_x = x if kx == 0 else 1 - x
        ref[...] = out_s[pl.ds(pl.multiple_of(2 * to_x * line, line), 2 * line)]
    grad_act = cot_s[:own].astype(F32)
    grad_act = grad_act + mm_t(grad_q, wq[...])
    grad_act = grad_act + mm_t((gk_s[...] * scale).astype(BF16), wk[...])
    grad_act = grad_act + mm_t(gv_s[...].astype(BF16), wv[...])
    convf, inverse, normed = norm_parts(conv_s[:own], gain)
    sigma = 1.0 / (1.0 + jnp.exp(-normed))
    scaled = grad_act * sigma * (1.0 + normed * (1.0 - sigma)) * gain
    mean = jnp.mean(scaled * convf, axis=-1, keepdims=True)
    grad_conv = inverse * (scaled - convf * inverse * inverse * mean)
    row = lax.broadcasted_iota(jnp.int32, grad_conv.shape, 0)
    first = jnp.where(q == 0, line, 0)
    last = jnp.where(q == 3, own - line, own)
    inside = jnp.logical_and(row >= first, row < last)
    grad_s[...] = jnp.where(inside, grad_conv, 0.0).astype(BF16)
    for kx, ref in ((0, grad0), (1, grad1)):
        to_x = x if kx == 0 else 1 - x
        ref[...] = grad_s[pl.ds(pl.multiple_of(2 * to_x * line, line), 4 * line)]


def attention(place, convs, cots, gain, wq, wk, wv, wo):
    block, chans = convs[0].shape[0] // 2, convs[0].shape[1]
    own, whole = 3 * block, 8 * block
    act = lambda n, t=BF16: pltpu.VMEM((n, chans), t)
    return pl.pallas_call(
        attention_kernel,
        in_specs=[SM] + [VM] * (len(convs) + len(cots) + 5),
        out_specs=[VM] * 4,
        out_shape=[jax.ShapeDtypeStruct((n * block, chans), BF16) for n in (1, 1, 2, 2)],
        scratch_shapes=[act(whole), act(whole), act(own)]
        + [act(whole)] * 4
        + [act(own, F32), act(own, F32), act(2 * block), act(own)],
        compiler_params=pltpu.CompilerParams(vmem_limit_bytes=26 * MIB),
        cost_estimate=pl.CostEstimate(
            flops=4 * 10**9, bytes_accessed=4 * 10**6, transcendentals=1 << 20
        ),
        name="attention",
    )(place, *convs, *cots, gain, wq, wk, wv, wo)


def site(h, c, y, x):
    return (h * 2 + c) * 8 + 2 * y + x


def send(value, runs, to):
    pairs = []
    for h in range(runs // 2):
        for c in range(2):
            for y in range(4):
                for x in range(2):
                    there = to(c, y, x)
                    if there is not None:
                        pairs.append((site(h, c, y, x), site(h, *there)))
    return lax.ppermute(value, ("tm", "rows"), pairs)


def home(ky, kx):
    return lambda c, y, x: (y % 2, 2 * ((y // 2 + ky) % 2) + c, x ^ kx)


def swap(c, y, x):
    return 1 - c, y, x


def across(c, y, x):
    return c, y, x ^ 1


def beyond(c, y, x):
    y = y + 1 if x else y - 1
    return (c, y, x ^ 1) if 0 <= y < 4 else None


def straight(c, y, x):
    y = y + 1 if x else y - 1
    return (c, y, x) if 0 <= y < 4 else None


def local(video, conv_weight, norm_gain, w_query, w_key, w_value, w_out, cotangent):
    frames, height, width, chans = video.shape
    runs, slabs = lax.axis_size("tm"), lax.axis_size("rows")
    assert (frames, height, slabs) == (2, 2, 8)
    slab_at = lax.axis_index("rows")
    x = slab_at % 2
    quarter = 2 * (slab_at // 4) + lax.axis_index("tm") % 2
    place = jnp.stack([x, quarter]).astype(jnp.int32)
    block = 2 * width

    edge = lax.dynamic_index_in_dim(video, x, 1, keepdims=False).reshape(block, chans)
    mine = video.reshape(2 * block, chans)
    far_other = send(edge, runs, beyond)
    packet = send(mine, runs, across)
    far_same = send(edge, runs, straight)
    cot_b = send(cotangent.reshape(2, block, chans), runs, home(0, 0))
    weight = load(conv_weight)
    cot_same = lax.dynamic_index_in_dim(cot_b, x, 0, keepdims=False)
    cot_other = lax.dynamic_index_in_dim(cot_b, 1 - x, 0, keepdims=False)
    quad = (2 * block, chans)
    for_next, taps = call(
        next_kernel, (place, mine, packet, far_same, far_other, weight), [SM] + [VM] * 5,
        [(quad, BF16), ((2, 6, width, 3 * chans), BF16)], [pltpu.VMEM(quad, F32)],
        24 * MIB, 10**9,
    )
    cached = lax.ppermute(for_next, "tm", [(i, i + 1) for i in range(runs - 1)])
    cot_other = send(cot_other, runs, across)
    own = call(
        own_kernel, (place, taps, weight), [SM, VM, VM], [(quad, F32)], [],
        24 * MIB, 10**9,
    )[0]
    cot_b = join(place, cot_same, cot_other)
    cot_c = send(cot_b, runs, lambda c, y, x: (c, y ^ 2, x))
    conv = (own + cached.astype(F32)).astype(BF16)
    conv_c = send(conv, runs, home(1, 0))
    conv_b = send(conv, runs, home(0, 0))
    cots = (cot_b, cot_c, send(cot_b, runs, swap), send(cot_c, runs, swap))
    convs = (conv_b, conv_c, send(conv_b, runs, swap), send(conv_c, runs, swap))
    out0, out1, grad0, grad1 = attention(
        place, convs, cots, norm_gain.reshape(1, chans), w_query, w_key, w_value, w_out
    )
    grad1 = send(grad1, runs, home(0, 1))
    grad0 = send(grad0, runs, home(0, 0))
    out1 = send(out1, runs, home(0, 1))
    out0 = send(out0, runs, home(0, 0))

    def backward(main, side, src, dst, dtype):
        kernel = functools.partial(backward_kernel, main, side, src, dst)
        return conv_call(kernel, place, slab, weight, width, dtype)

    slab = (grad0, grad1)
    for_last = backward(0, 1, 0, 1, BF16)
    handed = lax.ppermute(for_last, "tm", [(i + 1, i) for i in range(runs - 1)])
    own_grad, block_out = call(
        last_kernel, (place, grad0, grad1, out0, out1, weight), [SM] + [VM] * 5,
        [((2, block, chans), F32), ((2, block, chans), BF16)],
        [pltpu.VMEM((2, 4, width, 3 * chans), BF16), pltpu.SemaphoreType.DMA((2,))],
        24 * MIB, 10**9, outs=(VM, HBM),
    )
    video_grad = finish(own_grad, handed)
    return block_out.reshape(video.shape), video_grad.reshape(video.shape)


def solution(mesh):
    spec = P("tm", "rows", None, None)
    return jax.shard_map(
        local,
        mesh=mesh,
        in_specs=(spec, P(), P(), P(), P(), P(), P(), spec),
        out_specs=(spec, spec),
        check_vma=False,
    )
```

```python
import jax
import jax.numpy as jnp
from jax import lax
from jax.experimental import pallas as pl
from jax.experimental.pallas import tpu as pltpu
from jax.sharding import PartitionSpec as P


F32 = jnp.float32
BF16 = jnp.bfloat16
MIB = 1024 * 1024
LOG2E = 1.4426950408889634
LOAD = 44 * MIB
NEXT = 42 * MIB
VM = pl.BlockSpec(memory_space=pltpu.VMEM)
SM = pl.BlockSpec(memory_space=pltpu.SMEM)
HBM = pl.BlockSpec(memory_space=pltpu.HBM)


def call(kernel, operands, specs, shapes, scratch, limit, cost=0, outs=VM):
    return pl.pallas_call(
        kernel,
        in_specs=specs,
        out_specs=list(outs) if isinstance(outs, tuple) else [outs] * len(shapes),
        out_shape=[jax.ShapeDtypeStruct(dims, dtype) for dims, dtype in shapes],
        scratch_shapes=scratch,
        compiler_params=pltpu.CompilerParams(vmem_limit_bytes=limit),
        cost_estimate=pl.CostEstimate(flops=cost, bytes_accessed=1 << 20, transcendentals=0),
    )(*operands)


def join_kernel(place, same, other, out):
    x = place[0]
    half = same.shape[0]
    out[pl.ds(pl.multiple_of(x * half, half), half)] = same[...]
    out[pl.ds(pl.multiple_of((1 - x) * half, half), half)] = other[...]


def join(place, same, other):
    shape = (2 * same.shape[0], same.shape[1])
    return call(join_kernel, (place, same, other), [SM, VM, VM], [(shape, BF16)], [], 4 * MIB)[0]


def load_kernel(w_hbm, w_out, sem):
    copy = pltpu.make_async_copy(w_hbm.at[0:2], w_out, sem)
    copy.start()
    copy.wait()


def load(weight):
    return call(
        load_kernel, (weight,), [HBM], [((2,) + weight.shape[1:], weight.dtype)],
        [pltpu.SemaphoreType.DMA], LOAD,
    )[0]


def finish_kernel(own, handed, video_grad, total, sems):
    copies = []
    for f in range(2):
        total[f] = (own[f] + handed[f].astype(F32)).astype(BF16)
        copies.append(pltpu.make_async_copy(total.at[f], video_grad.at[f], sems.at[f]))
        copies[f].start()
    for copy in copies:
        copy.wait()


def finish(own, handed):
    return call(
        finish_kernel, (own, handed), [VM, VM], [(own.shape, BF16)],
        [pltpu.VMEM(own.shape, BF16), pltpu.SemaphoreType.DMA((2,))], 8 * MIB, outs=HBM,
    )[0]


def spread(rows_f32, width):
    n = rows_f32.shape[0]
    col = lax.broadcasted_iota(jnp.int32, rows_f32.shape, 0) % width
    left = jnp.where(col == 0, 0.0, pltpu.roll(rows_f32, 1, 0))
    right = jnp.where(col == width - 1, 0.0, pltpu.roll(rows_f32, n - 1, 0))
    return left, rows_f32, right


def fill(taps, frame, row, block, width, flip):
    n, _, chans = block.shape
    shifted = spread(block.astype(F32).reshape(n * width, chans), width)
    if flip:
        shifted = shifted[::-1]
    for c in range(3):
        taps[frame, row : row + n, :, c * chans : (c + 1) * chans] = (
            shifted[c].astype(BF16).reshape(n, width, chans)
        )


def conv_steps(taps, w_main, w_side, out, src, dst):
    def times(lhs, w_ref, b):
        return mm_t(lhs, jnp.concatenate([w_ref[b, c] for c in range(3)], axis=1))

    both = extra = None
    for b in range(3):
        row = 2 - b
        lhs = [taps[f, row : row + 2] for f in range(2)]
        lhs = [v.reshape(v.shape[0] * v.shape[1], v.shape[2]) for v in lhs]
        term = times(jnp.concatenate(lhs, axis=0), w_main, b)
        both = term if both is None else both + term
        term = times(lhs[src], w_side, b)
        extra = term if extra is None else extra + term
    half = both.shape[0] // 2
    for f in range(2):
        term = both[f * half : (f + 1) * half]
        out[f] = (term + extra if f == dst else term).astype(out.dtype)


def frame_taps(taps, frame, rows):
    piece = taps[frame, rows : rows + 4]
    return piece.reshape(piece.shape[0] * piece.shape[1], piece.shape[2])


def frame_conv(taps, w_ref, frame):
    chans = w_ref.shape[-1]
    total = None
    for b in range(3):
        term = mm(frame_taps(taps, frame, b), w_ref[b].reshape(3 * chans, chans))
        total = term if total is None else total + term
    return total


def next_kernel(place, mine, packet, far_same, far_other, w_ref, w_hbm, out, taps, w_last, acc, sem):
    copy = pltpu.make_async_copy(w_hbm.at[2], w_last, sem)
    copy.start()
    x = place[0]
    flip = x == 1
    width = taps.shape[2]
    chans = w_ref.shape[-1]
    for f in range(2):
        line = slice(f * width, (f + 1) * width)
        pair = slice(2 * f * width, 2 * (f + 1) * width)
        a, b = mine[pair], packet[pair]
        top = jnp.where(flip, far_same[line], far_other[line])
        bottom = jnp.where(flip, far_other[line], far_same[line])
        for row, rows in (
            (0, top), (1, jnp.where(flip, b, a)), (3, jnp.where(flip, a, b)), (5, bottom)
        ):
            fill(taps, f, row, rows.reshape(-1, width, chans), width, False)
    acc[...] = frame_conv(taps, w_ref.at[0], x)

    @pl.when(x == 0)
    def _():
        acc[...] += frame_conv(taps, w_ref.at[1], 1)

    out[...] = acc[...].astype(out.dtype)
    copy.wait()


def own_kernel(place, taps, w_ref, w_last, out):
    x = place[0]
    out[...] = frame_conv(taps, w_last, x)

    @pl.when(x == 1)
    def _():
        out[...] += frame_conv(taps, w_ref.at[1], 0)


def fill_slab(place, taps, r0, r1):
    width, chans = taps.shape[2], r0.shape[-1]
    swapped = place[0] == 1
    for f, (a, b) in enumerate(((r0, r1), (r1, r0))):
        rows = jnp.where(swapped, b[...], a[...])
        fill(taps, f, 0, rows.reshape(4, width, chans), width, True)


def grad_last_kernel(place, r0, r1, w_ref, out, taps):
    fill_slab(place, taps, r0, r1)
    conv_steps(taps, w_ref.at[0], w_ref.at[1], out, 0, 1)


def grad_own_kernel(place, r0, r1, out0, out1, w_ref, w_last, out, block_out, taps, sems):
    x = place[0]
    copies = [
        pltpu.make_async_copy(out0, block_out.at[x], sems.at[0]),
        pltpu.make_async_copy(out1, block_out.at[1 - x], sems.at[1]),
    ]
    for copy in copies:
        copy.start()
    fill_slab(place, taps, r0, r1)
    conv_steps(taps, w_last, w_ref.at[1], out, 1, 0)
    for copy in copies:
        copy.wait()


def norm_parts(conv, gain):
    convf = conv.astype(F32)
    inverse = lax.rsqrt(jnp.mean(convf * convf, axis=-1, keepdims=True) + 1e-06)
    normed = convf * inverse * gain
    return convf, inverse, normed


def mm(a, b):
    return jnp.dot(a, b, preferred_element_type=F32)


def mm_t(a, b):
    return lax.dot_general(a, b, (((1,), (1,)), ((), ())), preferred_element_type=F32)


def t_mm(a, b):
    return lax.dot_general(a, b, (((0,), (0,)), ((), ())), preferred_element_type=F32)


CHUNKS = ((0, 384), (384, 256), (640, 256), (896, 128))


def attention_kernel(
    place, c0, c2, c1, c3, t0, t2, t1, t3, gain_ref, wq, wk, wv, wo,
    out0, out1, grad0, grad1, conv_s, cot_s, act_s, q_s, k_s, v_s, g_s, gk_s, gv_s, out_s, grad_s,
):
    x, q = place[0], place[1]
    line = c0.shape[0] // 4
    own = 6 * line
    chans = wq.shape[0]
    scale = 1.0 / jnp.sqrt(jnp.float32(chans))
    gain = gain_ref[...]
    side = q + 1 - 2 * (q % 2)
    quarters = (q, (q + 2) % 4, side, (side + 2) % 4)
    for dst, refs in ((conv_s, (c0, c2, c1, c3)), (cot_s, (t0, t2, t1, t3))):
        for ref, quarter in zip(refs, quarters):
            for j in range(4):
                slot = (4 * (quarter - q) + j + 17) % 16
                dst[pl.ds(pl.multiple_of(slot * line, line), line)] = ref[j * line : (j + 1) * line]

    def activation(at, n):
        _, _, normed = norm_parts(conv_s[at : at + n], gain)
        return (normed / (1.0 + jnp.exp(-normed))).astype(BF16)

    coming = activation(*CHUNKS[0])
    act_s[...] = coming
    for i, (at, n) in enumerate(CHUNKS):
        rows = slice(at, at + n)
        act = coming
        if i + 1 < len(CHUNKS):
            coming = activation(*CHUNKS[i + 1])
        q_s[rows] = mm(act, wq[...]).astype(BF16)
        k_s[rows] = mm(act, wk[...]).astype(BF16)
        v_s[rows] = mm(act, wv[...]).astype(BF16)
        g_s[rows] = mm_t(cot_s[rows], wo[...]).astype(BF16)
    attended = grad_q = None

    def products(at, n):
        rows = slice(at, at + n)
        return mm_t(q_s[rows], k_s[...]), mm_t(g_s[rows], v_s[...])

    ahead = products(*CHUNKS[0])
    for i, (at, n) in enumerate(CHUNKS):
        rows = slice(at, at + n)
        scores, dprob = ahead
        if i + 1 < len(CHUNKS):
            ahead = products(*CHUNKS[i + 1])
        top = jnp.max(scores, axis=-1, keepdims=True)
        expo = jnp.exp2((scores - top) * (scale * LOG2E))
        inv_total = 1.0 / jnp.sum(expo, axis=-1, keepdims=True)
        delta = jnp.sum(expo * dprob, axis=-1, keepdims=True) * inv_total
        if at == 0:
            probs = expo * inv_total
            probs_b = probs.astype(BF16)
            mid = slice(line, own - line)
            attended = mm(probs_b[mid], v_s[...]).astype(BF16)
            dscore = (probs * (dprob - delta)).astype(BF16)
            grad_q = (mm(dscore, k_s[...]) * scale).astype(BF16)
            gk_s[...] = t_mm(dscore[:, :own], q_s[rows])
            gv_s[...] = t_mm(probs_b[:, :own], g_s[rows])
        else:
            probs = expo[:, :own] * inv_total
            dscore = (probs * (dprob[:, :own] - delta)).astype(BF16)
            gk_s[...] += t_mm(dscore, q_s[rows])
            gv_s[...] += t_mm(probs.astype(BF16), g_s[rows])
    out_s[...] = (act_s[line : own - line].astype(F32) + mm(attended, wo[...])).astype(BF16)
    for kx, ref in ((0, out0), (1, out1)):
        to_x = x if kx == 0 else 1 - x
        ref[...] = out_s[pl.ds(pl.multiple_of(2 * to_x * line, line), 2 * line)]
    grad_act = cot_s[:own].astype(F32)
    grad_act = grad_act + mm_t(grad_q, wq[...])
    grad_act = grad_act + mm_t((gk_s[...] * scale).astype(BF16), wk[...])
    grad_act = grad_act + mm_t(gv_s[...].astype(BF16), wv[...])
    convf, inverse, normed = norm_parts(conv_s[:own], gain)
    sigma = 1.0 / (1.0 + jnp.exp(-normed))
    scaled = grad_act * sigma * (1.0 + normed * (1.0 - sigma)) * gain
    mean = jnp.mean(scaled * convf, axis=-1, keepdims=True)
    grad_conv = inverse * (scaled - convf * inverse * inverse * mean)
    row = lax.broadcasted_iota(jnp.int32, grad_conv.shape, 0)
    first = jnp.where(q == 0, line, 0)
    last = jnp.where(q == 3, own - line, own)
    inside = jnp.logical_and(row >= first, row < last)
    grad_s[...] = jnp.where(inside, grad_conv, 0.0).astype(BF16)
    for kx, ref in ((0, grad0), (1, grad1)):
        to_x = x if kx == 0 else 1 - x
        ref[...] = grad_s[pl.ds(pl.multiple_of(2 * to_x * line, line), 4 * line)]


def attention(place, convs, cots, gain, wq, wk, wv, wo):
    block, chans = convs[0].shape[0] // 2, convs[0].shape[1]
    own, whole = 3 * block, 8 * block
    act = lambda n, t=BF16: pltpu.VMEM((n, chans), t)
    return pl.pallas_call(
        attention_kernel,
        in_specs=[SM] + [VM] * (len(convs) + len(cots) + 5),
        out_specs=[VM] * 4,
        out_shape=[jax.ShapeDtypeStruct((n * block, chans), BF16) for n in (1, 1, 2, 2)],
        scratch_shapes=[act(whole), act(whole), act(own)]
        + [act(whole)] * 4
        + [act(own, F32), act(own, F32), act(2 * block), act(own)],
        compiler_params=pltpu.CompilerParams(vmem_limit_bytes=26 * MIB),
        cost_estimate=pl.CostEstimate(
            flops=4 * 10**9, bytes_accessed=4 * 10**6, transcendentals=1 << 20
        ),
        name="attention",
    )(place, *convs, *cots, gain, wq, wk, wv, wo)


def site(h, c, y, x):
    return (h * 2 + c) * 8 + 2 * y + x


def send(value, runs, to):
    pairs = []
    for h in range(runs // 2):
        for c in range(2):
            for y in range(4):
                for x in range(2):
                    there = to(c, y, x)
                    if there is not None:
                        pairs.append((site(h, c, y, x), site(h, *there)))
    return lax.ppermute(value, ("tm", "rows"), pairs)


def home(ky, kx):
    return lambda c, y, x: (y % 2, 2 * ((y // 2 + ky) % 2) + c, x ^ kx)


def swap(c, y, x):
    return 1 - c, y, x


def across(c, y, x):
    return c, y, x ^ 1


def beyond(c, y, x):
    y = y + 1 if x else y - 1
    return (c, y, x ^ 1) if 0 <= y < 4 else None


def straight(c, y, x):
    y = y + 1 if x else y - 1
    return (c, y, x) if 0 <= y < 4 else None


def local(video, conv_weight, norm_gain, w_query, w_key, w_value, w_out, cotangent):
    frames, height, width, chans = video.shape
    runs, slabs = lax.axis_size("tm"), lax.axis_size("rows")
    assert (frames, height, slabs) == (2, 2, 8)
    slab_at = lax.axis_index("rows")
    x = slab_at % 2
    quarter = 2 * (slab_at // 4) + lax.axis_index("tm") % 2
    place = jnp.stack([x, quarter]).astype(jnp.int32)
    block = 2 * width

    edge = lax.dynamic_index_in_dim(video, x, 1, keepdims=False).reshape(block, chans)
    mine = video.reshape(2 * block, chans)
    far_other = send(edge, runs, beyond)
    packet = send(mine, runs, across)
    far_same = send(edge, runs, straight)
    cot_b = send(cotangent.reshape(2, block, chans), runs, home(0, 0))
    weight = load(conv_weight)
    cot_same = lax.dynamic_index_in_dim(cot_b, x, 0, keepdims=False)
    cot_other = lax.dynamic_index_in_dim(cot_b, 1 - x, 0, keepdims=False)
    cot_other = send(cot_other, runs, across)
    quad = (2 * block, chans)
    for_next, taps, w_last = call(
        next_kernel, (place, mine, packet, far_same, far_other, weight, conv_weight),
        [SM] + [VM] * 5 + [HBM],
        [(quad, BF16), ((2, 6, width, 3 * chans), BF16), (conv_weight.shape[1:], BF16)],
        [pltpu.VMEM(quad, F32), pltpu.SemaphoreType.DMA],
        NEXT, 10**9,
    )
    cached = lax.ppermute(for_next, "tm", [(i, i + 1) for i in range(runs - 1)])
    cot_b = join(place, cot_same, cot_other)
    cot_c = send(cot_b, runs, lambda c, y, x: (c, y ^ 2, x))
    own = call(
        own_kernel, (place, taps, weight, w_last), [SM, VM, VM, VM], [(quad, F32)], [],
        24 * MIB, 10**9,
    )[0]
    conv = (own + cached.astype(F32)).astype(BF16)
    conv_c = send(conv, runs, home(1, 0))
    conv_b = send(conv, runs, home(0, 0))
    cots = (cot_b, cot_c, send(cot_b, runs, swap), send(cot_c, runs, swap))
    convs = (conv_b, conv_c, send(conv_b, runs, swap), send(conv_c, runs, swap))
    out0, out1, grad0, grad1 = attention(
        place, convs, cots, norm_gain.reshape(1, chans), w_query, w_key, w_value, w_out
    )
    grad1 = send(grad1, runs, home(0, 1))
    grad0 = send(grad0, runs, home(0, 0))
    out1 = send(out1, runs, home(0, 1))
    out0 = send(out0, runs, home(0, 0))

    for_last = call(
        grad_last_kernel, (place, grad0, grad1, weight), [SM, VM, VM, VM],
        [((2, block, chans), BF16)], [pltpu.VMEM((2, 4, width, 3 * chans), BF16)],
        24 * MIB, 10**9,
    )[0]
    handed = lax.ppermute(for_last, "tm", [(i + 1, i) for i in range(runs - 1)])
    own_grad, block_out = call(
        grad_own_kernel, (place, grad0, grad1, out0, out1, weight, w_last), [SM] + [VM] * 6,
        [((2, block, chans), F32), ((2, block, chans), BF16)],
        [pltpu.VMEM((2, 4, width, 3 * chans), BF16), pltpu.SemaphoreType.DMA((2,))],
        24 * MIB, 10**9, outs=(VM, HBM),
    )
    video_grad = finish(own_grad, handed)
    return block_out.reshape(video.shape), video_grad.reshape(video.shape)


def solution(mesh):
    spec = P("tm", "rows", None, None)
    return jax.shard_map(
        local,
        mesh=mesh,
        in_specs=(spec, P(), P(), P(), P(), P(), P(), spec),
        out_specs=(spec, spec),
        check_vma=False,
    )
```

```python
import jax
import jax.numpy as jnp
from jax import lax
from jax.experimental import pallas as pl
from jax.experimental.pallas import tpu as pltpu
from jax.sharding import PartitionSpec as P


F32 = jnp.float32
BF16 = jnp.bfloat16
MIB = 1024 * 1024
LOG2E = 1.4426950408889634
LOAD = 44 * MIB
NEXT = 42 * MIB
VM = pl.BlockSpec(memory_space=pltpu.VMEM)
SM = pl.BlockSpec(memory_space=pltpu.SMEM)
HBM = pl.BlockSpec(memory_space=pltpu.HBM)


def call(kernel, operands, specs, shapes, scratch, limit, cost=0, outs=VM):
    return pl.pallas_call(
        kernel,
        in_specs=specs,
        out_specs=list(outs) if isinstance(outs, tuple) else [outs] * len(shapes),
        out_shape=[jax.ShapeDtypeStruct(dims, dtype) for dims, dtype in shapes],
        scratch_shapes=scratch,
        compiler_params=pltpu.CompilerParams(vmem_limit_bytes=limit),
        cost_estimate=pl.CostEstimate(flops=cost, bytes_accessed=1 << 20, transcendentals=0),
    )(*operands)


def join_kernel(place, same, other, out):
    x = place[0]
    half = same.shape[0]
    out[pl.ds(pl.multiple_of(x * half, half), half)] = same[...]
    out[pl.ds(pl.multiple_of((1 - x) * half, half), half)] = other[...]


def join(place, same, other):
    shape = (2 * same.shape[0], same.shape[1])
    return call(join_kernel, (place, same, other), [SM, VM, VM], [(shape, BF16)], [], 4 * MIB)[0]


def load_kernel(w_hbm, w_out, sem):
    copy = pltpu.make_async_copy(w_hbm.at[0:2], w_out, sem)
    copy.start()
    copy.wait()


def load(weight):
    return call(
        load_kernel, (weight,), [HBM], [((2,) + weight.shape[1:], weight.dtype)],
        [pltpu.SemaphoreType.DMA], LOAD,
    )[0]


def finish_kernel(own, handed, video_grad, total, sems):
    copies = []
    for f in range(2):
        total[f] = (own[f] + handed[f].astype(F32)).astype(BF16)
        copies.append(pltpu.make_async_copy(total.at[f], video_grad.at[f], sems.at[f]))
        copies[f].start()
    for copy in copies:
        copy.wait()


def finish(own, handed):
    return call(
        finish_kernel, (own, handed), [VM, VM], [(own.shape, BF16)],
        [pltpu.VMEM(own.shape, BF16), pltpu.SemaphoreType.DMA((2,))], 8 * MIB, outs=HBM,
    )[0]


def spread(rows_f32, width):
    n = rows_f32.shape[0]
    col = lax.broadcasted_iota(jnp.int32, rows_f32.shape, 0) % width
    left = jnp.where(col == 0, 0.0, pltpu.roll(rows_f32, 1, 0))
    right = jnp.where(col == width - 1, 0.0, pltpu.roll(rows_f32, n - 1, 0))
    return left, rows_f32, right


def fill(taps, frame, row, block, width, flip):
    n, _, chans = block.shape
    shifted = spread(block.astype(F32).reshape(n * width, chans), width)
    if flip:
        shifted = shifted[::-1]
    for c in range(3):
        taps[frame, row : row + n, :, c * chans : (c + 1) * chans] = (
            shifted[c].astype(BF16).reshape(n, width, chans)
        )


def conv_steps(taps, w_main, w_side, out, src, dst):
    def times(lhs, w_ref, b):
        return mm_t(lhs, jnp.concatenate([w_ref[b, c] for c in range(3)], axis=1))

    both = extra = None
    for b in range(3):
        row = 2 - b
        lhs = [taps[f, row : row + 2] for f in range(2)]
        lhs = [v.reshape(v.shape[0] * v.shape[1], v.shape[2]) for v in lhs]
        term = times(jnp.concatenate(lhs, axis=0), w_main, b)
        both = term if both is None else both + term
        term = times(lhs[src], w_side, b)
        extra = term if extra is None else extra + term
    half = both.shape[0] // 2
    for f in range(2):
        term = both[f * half : (f + 1) * half]
        out[f] = (term + extra if f == dst else term).astype(out.dtype)


def frame_taps(taps, frame, rows):
    piece = taps[frame, rows : rows + 4]
    return piece.reshape(piece.shape[0] * piece.shape[1], piece.shape[2])


def frame_conv(taps, w_ref, frame):
    chans = w_ref.shape[-1]
    total = None
    for b in range(3):
        term = mm(frame_taps(taps, frame, b), w_ref[b].reshape(3 * chans, chans))
        total = term if total is None else total + term
    return total


def next_kernel(place, mine, packet, far_same, far_other, w_ref, w_hbm, out, taps, w_last, acc, sem):
    copy = pltpu.make_async_copy(w_hbm.at[2], w_last, sem)
    copy.start()
    x = place[0]
    flip = x == 1
    width = taps.shape[2]
    chans = w_ref.shape[-1]
    for f in range(2):
        line = slice(f * width, (f + 1) * width)
        pair = slice(2 * f * width, 2 * (f + 1) * width)
        a, b = mine[pair], packet[pair]
        top = jnp.where(flip, far_same[line], far_other[line])
        bottom = jnp.where(flip, far_other[line], far_same[line])
        for row, rows in (
            (0, top), (1, jnp.where(flip, b, a)), (3, jnp.where(flip, a, b)), (5, bottom)
        ):
            fill(taps, f, row, rows.reshape(-1, width, chans), width, False)
    acc[...] = frame_conv(taps, w_ref.at[0], x)

    @pl.when(x == 0)
    def _():
        acc[...] += frame_conv(taps, w_ref.at[1], 1)

    out[...] = acc[...].astype(out.dtype)
    copy.wait()


def own_kernel(place, taps, w_ref, w_last, out):
    x = place[0]
    out[...] = frame_conv(taps, w_last, x)

    @pl.when(x == 1)
    def _():
        out[...] += frame_conv(taps, w_ref.at[1], 0)


def fill_slab(place, taps, r0, r1):
    width, chans = taps.shape[2], r0.shape[-1]
    swapped = place[0] == 1
    for f, (a, b) in enumerate(((r0, r1), (r1, r0))):
        rows = jnp.where(swapped, b[...], a[...])
        fill(taps, f, 0, rows.reshape(4, width, chans), width, True)


def grad_last_kernel(place, r0, r1, w_ref, out, taps):
    fill_slab(place, taps, r0, r1)
    conv_steps(taps, w_ref.at[0], w_ref.at[1], out, 0, 1)


def grad_own_kernel(place, taps, out0, out1, w_ref, w_last, out, block_out, sems):
    x = place[0]
    copies = [
        pltpu.make_async_copy(out0, block_out.at[x], sems.at[0]),
        pltpu.make_async_copy(out1, block_out.at[1 - x], sems.at[1]),
    ]
    for copy in copies:
        copy.start()
    conv_steps(taps, w_last, w_ref.at[1], out, 1, 0)
    for copy in copies:
        copy.wait()


def norm_parts(conv, gain):
    convf = conv.astype(F32)
    inverse = lax.rsqrt(jnp.mean(convf * convf, axis=-1, keepdims=True) + 1e-06)
    normed = convf * inverse * gain
    return convf, inverse, normed


def mm(a, b):
    return jnp.dot(a, b, preferred_element_type=F32)


def mm_t(a, b):
    return lax.dot_general(a, b, (((1,), (1,)), ((), ())), preferred_element_type=F32)


def t_mm(a, b):
    return lax.dot_general(a, b, (((0,), (0,)), ((), ())), preferred_element_type=F32)


CHUNKS = ((0, 384), (384, 640))


def attention_kernel(
    place, c0, c2, c1, c3, t0, t2, t1, t3, gain_ref, wq, wk, wv, wo,
    out0, out1, grad0, grad1, conv_s, cot_s, act_s, q_s, k_s, v_s, g_s, gk_s, gv_s, out_s, grad_s,
):
    x, q = place[0], place[1]
    line = c0.shape[0] // 4
    own = 6 * line
    chans = wq.shape[0]
    scale = 1.0 / jnp.sqrt(jnp.float32(chans))
    gain = gain_ref[...]
    side = q + 1 - 2 * (q % 2)
    quarters = (q, (q + 2) % 4, side, (side + 2) % 4)
    for dst, refs in ((conv_s, (c0, c2, c1, c3)), (cot_s, (t0, t2, t1, t3))):
        for ref, quarter in zip(refs, quarters):
            for j in range(4):
                slot = (4 * (quarter - q) + j + 17) % 16
                dst[pl.ds(pl.multiple_of(slot * line, line), line)] = ref[j * line : (j + 1) * line]

    def activation(at, n):
        _, _, normed = norm_parts(conv_s[at : at + n], gain)
        return (normed / (1.0 + jnp.exp(-normed))).astype(BF16)

    coming = activation(*CHUNKS[0])
    act_s[...] = coming
    for i, (at, n) in enumerate(CHUNKS):
        rows = slice(at, at + n)
        act = coming
        if i + 1 < len(CHUNKS):
            coming = activation(*CHUNKS[i + 1])
        q_s[rows] = mm(act, wq[...]).astype(BF16)
        k_s[rows] = mm(act, wk[...]).astype(BF16)
        v_s[rows] = mm(act, wv[...]).astype(BF16)
        g_s[rows] = mm_t(cot_s[rows], wo[...]).astype(BF16)
    attended = grad_q = None

    def products(at, n):
        rows = slice(at, at + n)
        return mm_t(q_s[rows], k_s[...]), mm_t(g_s[rows], v_s[...])

    ahead = products(*CHUNKS[0])
    for i, (at, n) in enumerate(CHUNKS):
        rows = slice(at, at + n)
        scores, dprob = ahead
        if i + 1 < len(CHUNKS):
            ahead = products(*CHUNKS[i + 1])
        top = jnp.max(scores, axis=-1, keepdims=True)
        expo = jnp.exp2((scores - top) * (scale * LOG2E))
        inv_total = 1.0 / jnp.sum(expo, axis=-1, keepdims=True)
        delta = jnp.sum(expo * dprob, axis=-1, keepdims=True) * inv_total
        if at == 0:
            probs = expo * inv_total
            probs_b = probs.astype(BF16)
            mid = slice(line, own - line)
            attended = mm(probs_b[mid], v_s[...]).astype(BF16)
            dscore = (probs * (dprob - delta)).astype(BF16)
            grad_q = (mm(dscore, k_s[...]) * scale).astype(BF16)
            gk_s[...] = t_mm(dscore[:, :own], q_s[rows])
            gv_s[...] = t_mm(probs_b[:, :own], g_s[rows])
        else:
            probs = expo[:, :own] * inv_total
            dscore = (probs * (dprob[:, :own] - delta)).astype(BF16)
            gk_s[...] += t_mm(dscore, q_s[rows])
            gv_s[...] += t_mm(probs.astype(BF16), g_s[rows])
    out_s[...] = (act_s[line : own - line].astype(F32) + mm(attended, wo[...])).astype(BF16)
    for kx, ref in ((0, out0), (1, out1)):
        to_x = x if kx == 0 else 1 - x
        ref[...] = out_s[pl.ds(pl.multiple_of(2 * to_x * line, line), 2 * line)]
    grad_act = cot_s[:own].astype(F32)
    grad_act = grad_act + mm_t(grad_q, wq[...])
    grad_act = grad_act + mm_t((gk_s[...] * scale).astype(BF16), wk[...])
    grad_act = grad_act + mm_t(gv_s[...].astype(BF16), wv[...])
    convf, inverse, normed = norm_parts(conv_s[:own], gain)
    sigma = 1.0 / (1.0 + jnp.exp(-normed))
    scaled = grad_act * sigma * (1.0 + normed * (1.0 - sigma)) * gain
    mean = jnp.mean(scaled * convf, axis=-1, keepdims=True)
    grad_conv = inverse * (scaled - convf * inverse * inverse * mean)
    row = lax.broadcasted_iota(jnp.int32, grad_conv.shape, 0)
    first = jnp.where(q == 0, line, 0)
    last = jnp.where(q == 3, own - line, own)
    inside = jnp.logical_and(row >= first, row < last)
    grad_s[...] = jnp.where(inside, grad_conv, 0.0).astype(BF16)
    for kx, ref in ((0, grad0), (1, grad1)):
        to_x = x if kx == 0 else 1 - x
        ref[...] = grad_s[pl.ds(pl.multiple_of(2 * to_x * line, line), 4 * line)]


def attention(place, convs, cots, gain, wq, wk, wv, wo):
    block, chans = convs[0].shape[0] // 2, convs[0].shape[1]
    own, whole = 3 * block, 8 * block
    act = lambda n, t=BF16: pltpu.VMEM((n, chans), t)
    return pl.pallas_call(
        attention_kernel,
        in_specs=[SM] + [VM] * (len(convs) + len(cots) + 5),
        out_specs=[VM] * 4,
        out_shape=[jax.ShapeDtypeStruct((n * block, chans), BF16) for n in (1, 1, 2, 2)],
        scratch_shapes=[act(whole), act(whole), act(own)]
        + [act(whole)] * 4
        + [act(own, F32), act(own, F32), act(2 * block), act(own)],
        compiler_params=pltpu.CompilerParams(vmem_limit_bytes=26 * MIB),
        cost_estimate=pl.CostEstimate(
            flops=4 * 10**9, bytes_accessed=4 * 10**6, transcendentals=1 << 20
        ),
        name="attention",
    )(place, *convs, *cots, gain, wq, wk, wv, wo)


def site(h, c, y, x):
    return (h * 2 + c) * 8 + 2 * y + x


def send(value, runs, to):
    pairs = []
    for h in range(runs // 2):
        for c in range(2):
            for y in range(4):
                for x in range(2):
                    there = to(c, y, x)
                    if there is not None:
                        pairs.append((site(h, c, y, x), site(h, *there)))
    return lax.ppermute(value, ("tm", "rows"), pairs)


def home(ky, kx):
    return lambda c, y, x: (y % 2, 2 * ((y // 2 + ky) % 2) + c, x ^ kx)


def swap(c, y, x):
    return 1 - c, y, x


def across(c, y, x):
    return c, y, x ^ 1


def beyond(c, y, x):
    y = y + 1 if x else y - 1
    return (c, y, x ^ 1) if 0 <= y < 4 else None


def straight(c, y, x):
    y = y + 1 if x else y - 1
    return (c, y, x) if 0 <= y < 4 else None


def local(video, conv_weight, norm_gain, w_query, w_key, w_value, w_out, cotangent):
    frames, height, width, chans = video.shape
    runs, slabs = lax.axis_size("tm"), lax.axis_size("rows")
    assert (frames, height, slabs) == (2, 2, 8)
    slab_at = lax.axis_index("rows")
    x = slab_at % 2
    quarter = 2 * (slab_at // 4) + lax.axis_index("tm") % 2
    place = jnp.stack([x, quarter]).astype(jnp.int32)
    block = 2 * width

    edge = lax.dynamic_index_in_dim(video, x, 1, keepdims=False).reshape(block, chans)
    mine = video.reshape(2 * block, chans)
    far_other = send(edge, runs, beyond)
    packet = send(mine, runs, across)
    far_same = send(edge, runs, straight)
    cot_b = send(cotangent.reshape(2, block, chans), runs, home(0, 0))
    weight = load(conv_weight)
    cot_same = lax.dynamic_index_in_dim(cot_b, x, 0, keepdims=False)
    cot_other = lax.dynamic_index_in_dim(cot_b, 1 - x, 0, keepdims=False)
    cot_other = send(cot_other, runs, across)
    quad = (2 * block, chans)
    for_next, taps, w_last = call(
        next_kernel, (place, mine, packet, far_same, far_other, weight, conv_weight),
        [SM] + [VM] * 5 + [HBM],
        [(quad, BF16), ((2, 6, width, 3 * chans), BF16), (conv_weight.shape[1:], BF16)],
        [pltpu.VMEM(quad, F32), pltpu.SemaphoreType.DMA],
        NEXT, 10**9,
    )
    cached = lax.ppermute(for_next, "tm", [(i, i + 1) for i in range(runs - 1)])
    cot_b = join(place, cot_same, cot_other)
    cot_c = send(cot_b, runs, lambda c, y, x: (c, y ^ 2, x))
    own = call(
        own_kernel, (place, taps, weight, w_last), [SM, VM, VM, VM], [(quad, F32)], [],
        24 * MIB, 10**9,
    )[0]
    conv = (own + cached.astype(F32)).astype(BF16)
    conv_c = send(conv, runs, home(1, 0))
    conv_b = send(conv, runs, home(0, 0))
    cots = (cot_b, cot_c, send(cot_b, runs, swap), send(cot_c, runs, swap))
    convs = (conv_b, conv_c, send(conv_b, runs, swap), send(conv_c, runs, swap))
    out0, out1, grad0, grad1 = attention(
        place, convs, cots, norm_gain.reshape(1, chans), w_query, w_key, w_value, w_out
    )
    grad1 = send(grad1, runs, home(0, 1))
    grad0 = send(grad0, runs, home(0, 0))
    out1 = send(out1, runs, home(0, 1))
    out0 = send(out0, runs, home(0, 0))

    for_last, taps = call(
        grad_last_kernel, (place, grad0, grad1, weight), [SM, VM, VM, VM],
        [((2, block, chans), BF16), ((2, 4, width, 3 * chans), BF16)], [],
        24 * MIB, 10**9,
    )
    handed = lax.ppermute(for_last, "tm", [(i + 1, i) for i in range(runs - 1)])
    own_grad, block_out = call(
        grad_own_kernel, (place, taps, out0, out1, weight, w_last), [SM] + [VM] * 5,
        [((2, block, chans), F32), ((2, block, chans), BF16)],
        [pltpu.SemaphoreType.DMA((2,))],
        24 * MIB, 10**9, outs=(VM, HBM),
    )
    video_grad = finish(own_grad, handed)
    return block_out.reshape(video.shape), video_grad.reshape(video.shape)


def solution(mesh):
    spec = P("tm", "rows", None, None)
    return jax.shard_map(
        local,
        mesh=mesh,
        in_specs=(spec, P(), P(), P(), P(), P(), P(), spec),
        out_specs=(spec, spec),
        check_vma=False,
    )
```

```python
import jax
import jax.numpy as jnp
from jax import lax
from jax.experimental import pallas as pl
from jax.experimental.pallas import tpu as pltpu
from jax.sharding import PartitionSpec as P


F32 = jnp.float32
BF16 = jnp.bfloat16
MIB = 1024 * 1024
LOG2E = 1.4426950408889634
LOAD = 44 * MIB
NEXT = 42 * MIB


def seat():
    slab, run = lax.axis_index("rows"), lax.axis_index("tm")
    return lax.rem(slab, 2), 2 * lax.div(slab, 4) + lax.rem(run, 2)


VM = pl.BlockSpec(memory_space=pltpu.VMEM)
HBM = pl.BlockSpec(memory_space=pltpu.HBM)


def call(kernel, operands, specs, shapes, scratch, limit, cost=0, outs=VM):
    return pl.pallas_call(
        kernel,
        in_specs=specs,
        out_specs=list(outs) if isinstance(outs, tuple) else [outs] * len(shapes),
        out_shape=[jax.ShapeDtypeStruct(dims, dtype) for dims, dtype in shapes],
        scratch_shapes=scratch,
        compiler_params=pltpu.CompilerParams(vmem_limit_bytes=limit),
        cost_estimate=pl.CostEstimate(flops=cost, bytes_accessed=1 << 20, transcendentals=0),
    )(*operands)


def join_kernel(same, other, out):
    x, _ = seat()
    half = same.shape[0]
    out[pl.ds(pl.multiple_of(x * half, half), half)] = same[...]
    out[pl.ds(pl.multiple_of((1 - x) * half, half), half)] = other[...]


def join(same, other):
    shape = (2 * same.shape[0], same.shape[1])
    return call(join_kernel, (same, other), [VM, VM], [(shape, BF16)], [], 4 * MIB)[0]


def load_kernel(w_hbm, w_out, sem):
    copy = pltpu.make_async_copy(w_hbm.at[0:2], w_out, sem)
    copy.start()
    copy.wait()


def load(weight):
    return call(
        load_kernel, (weight,), [HBM], [((2,) + weight.shape[1:], weight.dtype)],
        [pltpu.SemaphoreType.DMA], LOAD,
    )[0]


def finish_kernel(own, handed, video_grad, total, sems):
    copies = []
    for f in range(2):
        total[f] = (own[f] + handed[f].astype(F32)).astype(BF16)
        copies.append(pltpu.make_async_copy(total.at[f], video_grad.at[f], sems.at[f]))
        copies[f].start()
    for copy in copies:
        copy.wait()


def finish(own, handed):
    return call(
        finish_kernel, (own, handed), [VM, VM], [(own.shape, BF16)],
        [pltpu.VMEM(own.shape, BF16), pltpu.SemaphoreType.DMA((2,))], 8 * MIB, outs=HBM,
    )[0]


def spread(rows_f32, width):
    n = rows_f32.shape[0]
    col = lax.broadcasted_iota(jnp.int32, rows_f32.shape, 0) % width
    left = jnp.where(col == 0, 0.0, pltpu.roll(rows_f32, 1, 0))
    right = jnp.where(col == width - 1, 0.0, pltpu.roll(rows_f32, n - 1, 0))
    return left, rows_f32, right


def fill(taps, frame, row, block, width, flip):
    n, _, chans = block.shape
    shifted = spread(block.astype(F32).reshape(n * width, chans), width)
    if flip:
        shifted = shifted[::-1]
    for c in range(3):
        taps[frame, row : row + n, :, c * chans : (c + 1) * chans] = (
            shifted[c].astype(BF16).reshape(n, width, chans)
        )


def conv_steps(taps, w_main, w_side, out, src, dst):
    def times(lhs, w_ref, b):
        return mm_t(lhs, jnp.concatenate([w_ref[b, c] for c in range(3)], axis=1))

    both = extra = None
    for b in range(3):
        row = 2 - b
        lhs = [taps[f, row : row + 2] for f in range(2)]
        lhs = [v.reshape(v.shape[0] * v.shape[1], v.shape[2]) for v in lhs]
        term = times(jnp.concatenate(lhs, axis=0), w_main, b)
        both = term if both is None else both + term
        term = times(lhs[src], w_side, b)
        extra = term if extra is None else extra + term
    half = both.shape[0] // 2
    for f in range(2):
        term = both[f * half : (f + 1) * half]
        out[f] = (term + extra if f == dst else term).astype(out.dtype)


def frame_taps(taps, frame, rows):
    piece = taps[frame, rows : rows + 4]
    return piece.reshape(piece.shape[0] * piece.shape[1], piece.shape[2])


def frame_conv(taps, w_ref, frame):
    chans = w_ref.shape[-1]
    total = None
    for b in range(3):
        term = mm(frame_taps(taps, frame, b), w_ref[b].reshape(3 * chans, chans))
        total = term if total is None else total + term
    return total


def next_kernel(mine, packet, far_same, far_other, w_ref, w_hbm, out, taps, w_last, acc, sem):
    copy = pltpu.make_async_copy(w_hbm.at[2], w_last, sem)
    copy.start()
    x, _ = seat()
    flip = x == 1
    width = taps.shape[2]
    chans = w_ref.shape[-1]
    for f in range(2):
        line = slice(f * width, (f + 1) * width)
        pair = slice(2 * f * width, 2 * (f + 1) * width)
        a, b = mine[pair], packet[pair]
        top = jnp.where(flip, far_same[line], far_other[line])
        bottom = jnp.where(flip, far_other[line], far_same[line])
        for row, rows in (
            (0, top), (1, jnp.where(flip, b, a)), (3, jnp.where(flip, a, b)), (5, bottom)
        ):
            fill(taps, f, row, rows.reshape(-1, width, chans), width, False)
    acc[...] = frame_conv(taps, w_ref.at[0], x)

    @pl.when(x == 0)
    def _():
        acc[...] += frame_conv(taps, w_ref.at[1], 1)

    out[...] = acc[...].astype(out.dtype)
    copy.wait()


def own_kernel(taps, w_ref, w_last, out):
    x, _ = seat()
    out[...] = frame_conv(taps, w_last, x)

    @pl.when(x == 1)
    def _():
        out[...] += frame_conv(taps, w_ref.at[1], 0)


def fill_slab(taps, r0, r1):
    width, chans = taps.shape[2], r0.shape[-1]
    swapped = seat()[0] == 1
    for f, (a, b) in enumerate(((r0, r1), (r1, r0))):
        rows = jnp.where(swapped, b[...], a[...])
        fill(taps, f, 0, rows.reshape(4, width, chans), width, True)


def grad_last_kernel(r0, r1, w_ref, out, taps):
    fill_slab(taps, r0, r1)
    conv_steps(taps, w_ref.at[0], w_ref.at[1], out, 0, 1)


def grad_own_kernel(taps, out0, out1, w_ref, w_last, out, block_out, sems):
    x, _ = seat()
    copies = [
        pltpu.make_async_copy(out0, block_out.at[x], sems.at[0]),
        pltpu.make_async_copy(out1, block_out.at[1 - x], sems.at[1]),
    ]
    for copy in copies:
        copy.start()
    conv_steps(taps, w_last, w_ref.at[1], out, 1, 0)
    for copy in copies:
        copy.wait()


def norm_parts(conv, gain):
    convf = conv.astype(F32)
    inverse = lax.rsqrt(jnp.mean(convf * convf, axis=-1, keepdims=True) + 1e-06)
    normed = convf * inverse * gain
    return convf, inverse, normed


def mm(a, b):
    return jnp.dot(a, b, preferred_element_type=F32)


def mm_t(a, b):
    return lax.dot_general(a, b, (((1,), (1,)), ((), ())), preferred_element_type=F32)


def t_mm(a, b):
    return lax.dot_general(a, b, (((0,), (0,)), ((), ())), preferred_element_type=F32)


CHUNKS = ((0, 384), (384, 640))


def attention_kernel(
    c0, c2, c1, c3, t0, t2, t1, t3, gain_ref, wq, wk, wv, wo,
    out0, out1, grad0, grad1, conv_s, cot_s, act_s, q_s, k_s, v_s, g_s, gk_s, gv_s, out_s, grad_s,
):
    x, q = seat()
    line = c0.shape[0] // 4
    own = 6 * line
    chans = wq.shape[0]
    scale = 1.0 / jnp.sqrt(jnp.float32(chans))
    gain = gain_ref[...]
    side = q + 1 - 2 * (q % 2)
    quarters = (q, (q + 2) % 4, side, (side + 2) % 4)
    for dst, refs in ((conv_s, (c0, c2, c1, c3)), (cot_s, (t0, t2, t1, t3))):
        for ref, quarter in zip(refs, quarters):
            for j in range(4):
                slot = (4 * (quarter - q) + j + 17) % 16
                dst[pl.ds(pl.multiple_of(slot * line, line), line)] = ref[j * line : (j + 1) * line]

    def activation(at, n):
        _, _, normed = norm_parts(conv_s[at : at + n], gain)
        return (normed / (1.0 + jnp.exp(-normed))).astype(BF16)

    coming = activation(*CHUNKS[0])
    act_s[...] = coming
    for i, (at, n) in enumerate(CHUNKS):
        rows = slice(at, at + n)
        act = coming
        if i + 1 < len(CHUNKS):
            coming = activation(*CHUNKS[i + 1])
        q_s[rows] = mm(act, wq[...]).astype(BF16)
        k_s[rows] = mm(act, wk[...]).astype(BF16)
        v_s[rows] = mm(act, wv[...]).astype(BF16)
        g_s[rows] = mm_t(cot_s[rows], wo[...]).astype(BF16)
    attended = grad_q = None

    def products(at, n):
        rows = slice(at, at + n)
        return mm_t(q_s[rows], k_s[...]), mm_t(g_s[rows], v_s[...])

    ahead = products(*CHUNKS[0])
    for i, (at, n) in enumerate(CHUNKS):
        rows = slice(at, at + n)
        scores, dprob = ahead
        if i + 1 < len(CHUNKS):
            ahead = products(*CHUNKS[i + 1])
        top = jnp.max(scores, axis=-1, keepdims=True)
        expo = jnp.exp2((scores - top) * (scale * LOG2E))
        inv_total = 1.0 / jnp.sum(expo, axis=-1, keepdims=True)
        delta = jnp.sum(expo * dprob, axis=-1, keepdims=True) * inv_total
        if at == 0:
            probs = expo * inv_total
            probs_b = probs.astype(BF16)
            mid = slice(line, own - line)
            attended = mm(probs_b[mid], v_s[...]).astype(BF16)
            dscore = (probs * (dprob - delta)).astype(BF16)
            grad_q = (mm(dscore, k_s[...]) * scale).astype(BF16)
            gk_s[...] = t_mm(dscore[:, :own], q_s[rows])
            gv_s[...] = t_mm(probs_b[:, :own], g_s[rows])
        else:
            probs = expo[:, :own] * inv_total
            dscore = (probs * (dprob[:, :own] - delta)).astype(BF16)
            gk_s[...] += t_mm(dscore, q_s[rows])
            gv_s[...] += t_mm(probs.astype(BF16), g_s[rows])
    out_s[...] = (act_s[line : own - line].astype(F32) + mm(attended, wo[...])).astype(BF16)
    for kx, ref in ((0, out0), (1, out1)):
        to_x = x if kx == 0 else 1 - x
        ref[...] = out_s[pl.ds(pl.multiple_of(2 * to_x * line, line), 2 * line)]
    grad_act = cot_s[:own].astype(F32)
    grad_act = grad_act + mm_t(grad_q, wq[...])
    grad_act = grad_act + mm_t((gk_s[...] * scale).astype(BF16), wk[...])
    grad_act = grad_act + mm_t(gv_s[...].astype(BF16), wv[...])
    convf, inverse, normed = norm_parts(conv_s[:own], gain)
    sigma = 1.0 / (1.0 + jnp.exp(-normed))
    scaled = grad_act * sigma * (1.0 + normed * (1.0 - sigma)) * gain
    mean = jnp.mean(scaled * convf, axis=-1, keepdims=True)
    grad_conv = inverse * (scaled - convf * inverse * inverse * mean)
    row = lax.broadcasted_iota(jnp.int32, grad_conv.shape, 0)
    first = jnp.where(q == 0, line, 0)
    last = jnp.where(q == 3, own - line, own)
    inside = jnp.logical_and(row >= first, row < last)
    grad_s[...] = jnp.where(inside, grad_conv, 0.0).astype(BF16)
    for kx, ref in ((0, grad0), (1, grad1)):
        to_x = x if kx == 0 else 1 - x
        ref[...] = grad_s[pl.ds(pl.multiple_of(2 * to_x * line, line), 4 * line)]


def attention(convs, cots, gain, wq, wk, wv, wo):
    block, chans = convs[0].shape[0] // 2, convs[0].shape[1]
    own, whole = 3 * block, 8 * block
    act = lambda n, t=BF16: pltpu.VMEM((n, chans), t)
    return pl.pallas_call(
        attention_kernel,
        in_specs=[VM] * (len(convs) + len(cots) + 5),
        out_specs=[VM] * 4,
        out_shape=[jax.ShapeDtypeStruct((n * block, chans), BF16) for n in (1, 1, 2, 2)],
        scratch_shapes=[act(whole), act(whole), act(own)]
        + [act(whole)] * 4
        + [act(own, F32), act(own, F32), act(2 * block), act(own)],
        compiler_params=pltpu.CompilerParams(vmem_limit_bytes=26 * MIB),
        cost_estimate=pl.CostEstimate(
            flops=4 * 10**9, bytes_accessed=4 * 10**6, transcendentals=1 << 20
        ),
        name="attention",
    )(*convs, *cots, gain, wq, wk, wv, wo)


def site(h, c, y, x):
    return (h * 2 + c) * 8 + 2 * y + x


def send(value, runs, to):
    pairs = []
    for h in range(runs // 2):
        for c in range(2):
            for y in range(4):
                for x in range(2):
                    there = to(c, y, x)
                    if there is not None:
                        pairs.append((site(h, c, y, x), site(h, *there)))
    return lax.ppermute(value, ("tm", "rows"), pairs)


def home(ky, kx):
    return lambda c, y, x: (y % 2, 2 * ((y // 2 + ky) % 2) + c, x ^ kx)


def swap(c, y, x):
    return 1 - c, y, x


def across(c, y, x):
    return c, y, x ^ 1


def beyond(c, y, x):
    y = y + 1 if x else y - 1
    return (c, y, x ^ 1) if 0 <= y < 4 else None


def straight(c, y, x):
    y = y + 1 if x else y - 1
    return (c, y, x) if 0 <= y < 4 else None


def local(video, conv_weight, norm_gain, w_query, w_key, w_value, w_out, cotangent):
    frames, height, width, chans = video.shape
    runs, slabs = lax.axis_size("tm"), lax.axis_size("rows")
    assert (frames, height, slabs) == (2, 2, 8)
    x, _ = seat()
    block = 2 * width

    edge = lax.dynamic_index_in_dim(video, x, 1, keepdims=False).reshape(block, chans)
    mine = video.reshape(2 * block, chans)
    far_other = send(edge, runs, beyond)
    packet = send(mine, runs, across)
    far_same = send(edge, runs, straight)
    cot_b = send(cotangent.reshape(2, block, chans), runs, home(0, 0))
    weight = load(conv_weight)
    cot_same = lax.dynamic_index_in_dim(cot_b, x, 0, keepdims=False)
    cot_other = lax.dynamic_index_in_dim(cot_b, 1 - x, 0, keepdims=False)
    cot_other = send(cot_other, runs, across)
    quad = (2 * block, chans)
    for_next, taps, w_last = call(
        next_kernel, (mine, packet, far_same, far_other, weight, conv_weight),
        [VM] * 5 + [HBM],
        [(quad, BF16), ((2, 6, width, 3 * chans), BF16), (conv_weight.shape[1:], BF16)],
        [pltpu.VMEM(quad, F32), pltpu.SemaphoreType.DMA],
        NEXT, 10**9,
    )
    cached = lax.ppermute(for_next, "tm", [(i, i + 1) for i in range(runs - 1)])
    cot_b = join(cot_same, cot_other)
    cot_c = send(cot_b, runs, lambda c, y, x: (c, y ^ 2, x))
    own = call(
        own_kernel, (taps, weight, w_last), [VM, VM, VM], [(quad, F32)], [],
        24 * MIB, 10**9,
    )[0]
    conv = (own + cached.astype(F32)).astype(BF16)
    conv_c = send(conv, runs, home(1, 0))
    conv_b = send(conv, runs, home(0, 0))
    cots = (cot_b, cot_c, send(cot_b, runs, swap), send(cot_c, runs, swap))
    convs = (conv_b, conv_c, send(conv_b, runs, swap), send(conv_c, runs, swap))
    out0, out1, grad0, grad1 = attention(
        convs, cots, norm_gain.reshape(1, chans), w_query, w_key, w_value, w_out
    )
    grad1 = send(grad1, runs, home(0, 1))
    grad0 = send(grad0, runs, home(0, 0))
    out1 = send(out1, runs, home(0, 1))
    out0 = send(out0, runs, home(0, 0))

    for_last, taps = call(
        grad_last_kernel, (grad0, grad1, weight), [VM, VM, VM],
        [((2, block, chans), BF16), ((2, 4, width, 3 * chans), BF16)], [],
        24 * MIB, 10**9,
    )
    handed = lax.ppermute(for_last, "tm", [(i + 1, i) for i in range(runs - 1)])
    own_grad, block_out = call(
        grad_own_kernel, (taps, out0, out1, weight, w_last), [VM] * 5,
        [((2, block, chans), F32), ((2, block, chans), BF16)],
        [pltpu.SemaphoreType.DMA((2,))],
        24 * MIB, 10**9, outs=(VM, HBM),
    )
    video_grad = finish(own_grad, handed)
    return block_out.reshape(video.shape), video_grad.reshape(video.shape)


def solution(mesh):
    spec = P("tm", "rows", None, None)
    return jax.shard_map(
        local,
        mesh=mesh,
        in_specs=(spec, P(), P(), P(), P(), P(), P(), spec),
        out_specs=(spec, spec),
        check_vma=False,
    )
```

```python
import jax
import jax.numpy as jnp
from jax import lax
from jax.experimental import pallas as pl
from jax.experimental.pallas import tpu as pltpu
from jax.sharding import PartitionSpec as P


F32 = jnp.float32
BF16 = jnp.bfloat16
MIB = 1024 * 1024
LOG2E = 1.4426950408889634
LOAD = 44 * MIB
NEXT = 42 * MIB


def seat():
    slab, run = lax.axis_index("rows"), lax.axis_index("tm")
    return lax.rem(slab, 2), 2 * lax.div(slab, 4) + lax.rem(run, 2)


VM = pl.BlockSpec(memory_space=pltpu.VMEM)
HBM = pl.BlockSpec(memory_space=pltpu.HBM)


def call(kernel, operands, specs, shapes, scratch, limit, cost=0, outs=VM):
    return pl.pallas_call(
        kernel,
        in_specs=specs,
        out_specs=list(outs) if isinstance(outs, tuple) else [outs] * len(shapes),
        out_shape=[jax.ShapeDtypeStruct(dims, dtype) for dims, dtype in shapes],
        scratch_shapes=scratch,
        compiler_params=pltpu.CompilerParams(vmem_limit_bytes=limit),
        cost_estimate=pl.CostEstimate(flops=cost, bytes_accessed=1 << 20, transcendentals=0),
    )(*operands)


def join_kernel(same, other, out):
    x, _ = seat()
    half = same.shape[0]
    out[pl.ds(pl.multiple_of(x * half, half), half)] = same[...]
    out[pl.ds(pl.multiple_of((1 - x) * half, half), half)] = other[...]


def join(same, other):
    shape = (2 * same.shape[0], same.shape[1])
    return call(join_kernel, (same, other), [VM, VM], [(shape, BF16)], [], 4 * MIB)[0]


def load_kernel(w_hbm, w_out, sem):
    copy = pltpu.make_async_copy(w_hbm.at[0:2], w_out, sem)
    copy.start()
    copy.wait()


def load(weight):
    return call(
        load_kernel, (weight,), [HBM], [((2,) + weight.shape[1:], weight.dtype)],
        [pltpu.SemaphoreType.DMA], LOAD,
    )[0]


def finish_kernel(own, handed, out0, out1, video_grad, block_out, total, sems):
    x, _ = seat()
    copies = [
        pltpu.make_async_copy(out0, block_out.at[x], sems.at[2]),
        pltpu.make_async_copy(out1, block_out.at[1 - x], sems.at[3]),
    ]
    for copy in copies:
        copy.start()
    for f in range(2):
        total[f] = (own[f] + handed[f].astype(F32)).astype(BF16)
        copies.append(pltpu.make_async_copy(total.at[f], video_grad.at[f], sems.at[f]))
        copies[-1].start()
    for copy in copies:
        copy.wait()


def finish(own, handed, out0, out1):
    return call(
        finish_kernel, (own, handed, out0, out1), [VM] * 4, [(own.shape, BF16)] * 2,
        [pltpu.VMEM(own.shape, BF16), pltpu.SemaphoreType.DMA((4,))], 8 * MIB, outs=HBM,
    )


def spread(rows_f32, width):
    n = rows_f32.shape[0]
    col = lax.broadcasted_iota(jnp.int32, rows_f32.shape, 0) % width
    left = jnp.where(col == 0, 0.0, pltpu.roll(rows_f32, 1, 0))
    right = jnp.where(col == width - 1, 0.0, pltpu.roll(rows_f32, n - 1, 0))
    return left, rows_f32, right


def fill(taps, frame, row, block, width, flip):
    n, _, chans = block.shape
    shifted = spread(block.astype(F32).reshape(n * width, chans), width)
    if flip:
        shifted = shifted[::-1]
    for c in range(3):
        taps[frame, row : row + n, :, c * chans : (c + 1) * chans] = (
            shifted[c].astype(BF16).reshape(n, width, chans)
        )


def conv_steps(taps, w_main, w_side, out, src, dst):
    def times(lhs, w_ref, b):
        return mm_t(lhs, jnp.concatenate([w_ref[b, c] for c in range(3)], axis=1))

    both = extra = None
    for b in range(3):
        row = 2 - b
        lhs = [taps[f, row : row + 2] for f in range(2)]
        lhs = [v.reshape(v.shape[0] * v.shape[1], v.shape[2]) for v in lhs]
        term = times(jnp.concatenate(lhs, axis=0), w_main, b)
        both = term if both is None else both + term
        term = times(lhs[src], w_side, b)
        extra = term if extra is None else extra + term
    half = both.shape[0] // 2
    for f in range(2):
        term = both[f * half : (f + 1) * half]
        out[f] = (term + extra if f == dst else term).astype(out.dtype)


def frame_taps(taps, frame, rows):
    piece = taps[frame, rows : rows + 4]
    return piece.reshape(piece.shape[0] * piece.shape[1], piece.shape[2])


def frame_conv(taps, w_ref, frame):
    chans = w_ref.shape[-1]
    total = None
    for b in range(3):
        term = mm(frame_taps(taps, frame, b), w_ref[b].reshape(3 * chans, chans))
        total = term if total is None else total + term
    return total


def next_kernel(mine, packet, far_same, far_other, w_ref, w_hbm, out, taps, w_last, acc, sem):
    copy = pltpu.make_async_copy(w_hbm.at[2], w_last, sem)
    copy.start()
    x, _ = seat()
    flip = x == 1
    width = taps.shape[2]
    chans = w_ref.shape[-1]
    for f in range(2):
        line = slice(f * width, (f + 1) * width)
        pair = slice(2 * f * width, 2 * (f + 1) * width)
        a, b = mine[pair], packet[pair]
        top = jnp.where(flip, far_same[line], far_other[line])
        bottom = jnp.where(flip, far_other[line], far_same[line])
        for row, rows in (
            (0, top), (1, jnp.where(flip, b, a)), (3, jnp.where(flip, a, b)), (5, bottom)
        ):
            fill(taps, f, row, rows.reshape(-1, width, chans), width, False)
    acc[...] = frame_conv(taps, w_ref.at[0], x)

    @pl.when(x == 0)
    def _():
        acc[...] += frame_conv(taps, w_ref.at[1], 1)

    out[...] = acc[...].astype(out.dtype)
    copy.wait()


def own_kernel(taps, w_ref, w_last, out):
    x, _ = seat()
    out[...] = frame_conv(taps, w_last, x)

    @pl.when(x == 1)
    def _():
        out[...] += frame_conv(taps, w_ref.at[1], 0)


def fill_slab(taps, r0, r1):
    width, chans = taps.shape[2], r0.shape[-1]
    swapped = seat()[0] == 1
    for f, (a, b) in enumerate(((r0, r1), (r1, r0))):
        rows = jnp.where(swapped, b[...], a[...])
        fill(taps, f, 0, rows.reshape(4, width, chans), width, True)


def grad_last_kernel(r0, r1, w_ref, out, taps):
    fill_slab(taps, r0, r1)
    conv_steps(taps, w_ref.at[0], w_ref.at[1], out, 0, 1)


def grad_own_kernel(taps, w_ref, w_last, out):
    conv_steps(taps, w_last, w_ref.at[1], out, 1, 0)


def norm_parts(conv, gain):
    convf = conv.astype(F32)
    inverse = lax.rsqrt(jnp.mean(convf * convf, axis=-1, keepdims=True) + 1e-06)
    normed = convf * inverse * gain
    return convf, inverse, normed


def mm(a, b):
    return jnp.dot(a, b, preferred_element_type=F32)


def mm_t(a, b):
    return lax.dot_general(a, b, (((1,), (1,)), ((), ())), preferred_element_type=F32)


def t_mm(a, b):
    return lax.dot_general(a, b, (((0,), (0,)), ((), ())), preferred_element_type=F32)


CHUNKS = ((0, 384), (384, 640))


def attention_kernel(
    c0, c2, c1, c3, t0, t2, t1, t3, gain_ref, wq, wk, wv, wo,
    out0, out1, grad0, grad1, conv_s, cot_s, act_s, q_s, k_s, v_s, g_s, gk_s, gv_s, out_s, grad_s,
):
    x, q = seat()
    line = c0.shape[0] // 4
    own = 6 * line
    chans = wq.shape[0]
    scale = 1.0 / jnp.sqrt(jnp.float32(chans))
    gain = gain_ref[...]
    side = q + 1 - 2 * (q % 2)
    quarters = (q, (q + 2) % 4, side, (side + 2) % 4)
    for dst, refs in ((conv_s, (c0, c2, c1, c3)), (cot_s, (t0, t2, t1, t3))):
        for ref, quarter in zip(refs, quarters):
            for j in range(4):
                slot = (4 * (quarter - q) + j + 17) % 16
                dst[pl.ds(pl.multiple_of(slot * line, line), line)] = ref[j * line : (j + 1) * line]

    def activation(at, n):
        _, _, normed = norm_parts(conv_s[at : at + n], gain)
        return (normed / (1.0 + jnp.exp(-normed))).astype(BF16)

    coming = activation(*CHUNKS[0])
    act_s[...] = coming
    for i, (at, n) in enumerate(CHUNKS):
        rows = slice(at, at + n)
        act = coming
        if i + 1 < len(CHUNKS):
            coming = activation(*CHUNKS[i + 1])
        q_s[rows] = mm(act, wq[...]).astype(BF16)
        k_s[rows] = mm(act, wk[...]).astype(BF16)
        v_s[rows] = mm(act, wv[...]).astype(BF16)
        g_s[rows] = mm_t(cot_s[rows], wo[...]).astype(BF16)
    attended = grad_q = None

    def products(at, n):
        rows = slice(at, at + n)
        return mm_t(q_s[rows], k_s[...]), mm_t(g_s[rows], v_s[...])

    ahead = products(*CHUNKS[0])
    for i, (at, n) in enumerate(CHUNKS):
        rows = slice(at, at + n)
        scores, dprob = ahead
        if i + 1 < len(CHUNKS):
            ahead = products(*CHUNKS[i + 1])
        top = jnp.max(scores, axis=-1, keepdims=True)
        expo = jnp.exp2((scores - top) * (scale * LOG2E))
        inv_total = 1.0 / jnp.sum(expo, axis=-1, keepdims=True)
        delta = jnp.sum(expo * dprob, axis=-1, keepdims=True) * inv_total
        if at == 0:
            probs = expo * inv_total
            probs_b = probs.astype(BF16)
            mid = slice(line, own - line)
            attended = mm(probs_b[mid], v_s[...]).astype(BF16)
            dscore = (probs * (dprob - delta)).astype(BF16)
            grad_q = (mm(dscore, k_s[...]) * scale).astype(BF16)
            gk_s[...] = t_mm(dscore[:, :own], q_s[rows])
            gv_s[...] = t_mm(probs_b[:, :own], g_s[rows])
        else:
            probs = expo[:, :own] * inv_total
            dscore = (probs * (dprob[:, :own] - delta)).astype(BF16)
            gk_s[...] += t_mm(dscore, q_s[rows])
            gv_s[...] += t_mm(probs.astype(BF16), g_s[rows])
    out_s[...] = (act_s[line : own - line].astype(F32) + mm(attended, wo[...])).astype(BF16)
    for kx, ref in ((0, out0), (1, out1)):
        to_x = x if kx == 0 else 1 - x
        ref[...] = out_s[pl.ds(pl.multiple_of(2 * to_x * line, line), 2 * line)]
    grad_act = cot_s[:own].astype(F32)
    grad_act = grad_act + mm_t(grad_q, wq[...])
    grad_act = grad_act + mm_t((gk_s[...] * scale).astype(BF16), wk[...])
    grad_act = grad_act + mm_t(gv_s[...].astype(BF16), wv[...])
    convf, inverse, normed = norm_parts(conv_s[:own], gain)
    sigma = 1.0 / (1.0 + jnp.exp(-normed))
    scaled = grad_act * sigma * (1.0 + normed * (1.0 - sigma)) * gain
    mean = jnp.mean(scaled * convf, axis=-1, keepdims=True)
    grad_conv = inverse * (scaled - convf * inverse * inverse * mean)
    row = lax.broadcasted_iota(jnp.int32, grad_conv.shape, 0)
    first = jnp.where(q == 0, line, 0)
    last = jnp.where(q == 3, own - line, own)
    inside = jnp.logical_and(row >= first, row < last)
    grad_s[...] = jnp.where(inside, grad_conv, 0.0).astype(BF16)
    for kx, ref in ((0, grad0), (1, grad1)):
        to_x = x if kx == 0 else 1 - x
        ref[...] = grad_s[pl.ds(pl.multiple_of(2 * to_x * line, line), 4 * line)]


def attention(convs, cots, gain, wq, wk, wv, wo):
    block, chans = convs[0].shape[0] // 2, convs[0].shape[1]
    own, whole = 3 * block, 8 * block
    act = lambda n, t=BF16: pltpu.VMEM((n, chans), t)
    return pl.pallas_call(
        attention_kernel,
        in_specs=[VM] * (len(convs) + len(cots) + 5),
        out_specs=[VM] * 4,
        out_shape=[jax.ShapeDtypeStruct((n * block, chans), BF16) for n in (1, 1, 2, 2)],
        scratch_shapes=[act(whole), act(whole), act(own)]
        + [act(whole)] * 4
        + [act(own, F32), act(own, F32), act(2 * block), act(own)],
        compiler_params=pltpu.CompilerParams(vmem_limit_bytes=26 * MIB),
        cost_estimate=pl.CostEstimate(
            flops=4 * 10**9, bytes_accessed=4 * 10**6, transcendentals=1 << 20
        ),
        name="attention",
    )(*convs, *cots, gain, wq, wk, wv, wo)


def site(h, c, y, x):
    return (h * 2 + c) * 8 + 2 * y + x


def send(value, runs, to):
    pairs = []
    for h in range(runs // 2):
        for c in range(2):
            for y in range(4):
                for x in range(2):
                    there = to(c, y, x)
                    if there is not None:
                        pairs.append((site(h, c, y, x), site(h, *there)))
    return lax.ppermute(value, ("tm", "rows"), pairs)


def home(ky, kx):
    return lambda c, y, x: (y % 2, 2 * ((y // 2 + ky) % 2) + c, x ^ kx)


def swap(c, y, x):
    return 1 - c, y, x


def across(c, y, x):
    return c, y, x ^ 1


def beyond(c, y, x):
    y = y + 1 if x else y - 1
    return (c, y, x ^ 1) if 0 <= y < 4 else None


def straight(c, y, x):
    y = y + 1 if x else y - 1
    return (c, y, x) if 0 <= y < 4 else None


def local(video, conv_weight, norm_gain, w_query, w_key, w_value, w_out, cotangent):
    frames, height, width, chans = video.shape
    runs, slabs = lax.axis_size("tm"), lax.axis_size("rows")
    assert (frames, height, slabs) == (2, 2, 8)
    x, _ = seat()
    block = 2 * width

    edge = lax.dynamic_index_in_dim(video, x, 1, keepdims=False).reshape(block, chans)
    mine = video.reshape(2 * block, chans)
    far_other = send(edge, runs, beyond)
    packet = send(mine, runs, across)
    far_same = send(edge, runs, straight)
    cot_b = send(cotangent.reshape(2, block, chans), runs, home(0, 0))
    weight = load(conv_weight)
    cot_same = lax.dynamic_index_in_dim(cot_b, x, 0, keepdims=False)
    cot_other = lax.dynamic_index_in_dim(cot_b, 1 - x, 0, keepdims=False)
    cot_other = send(cot_other, runs, across)
    quad = (2 * block, chans)
    for_next, taps, w_last = call(
        next_kernel, (mine, packet, far_same, far_other, weight, conv_weight),
        [VM] * 5 + [HBM],
        [(quad, BF16), ((2, 6, width, 3 * chans), BF16), (conv_weight.shape[1:], BF16)],
        [pltpu.VMEM(quad, F32), pltpu.SemaphoreType.DMA],
        NEXT, 10**9,
    )
    cached = lax.ppermute(for_next, "tm", [(i, i + 1) for i in range(runs - 1)])
    cot_b = join(cot_same, cot_other)
    cot_c = send(cot_b, runs, lambda c, y, x: (c, y ^ 2, x))
    own = call(
        own_kernel, (taps, weight, w_last), [VM, VM, VM], [(quad, F32)], [],
        24 * MIB, 10**9,
    )[0]
    conv = (own + cached.astype(F32)).astype(BF16)
    conv_c = send(conv, runs, home(1, 0))
    conv_b = send(conv, runs, home(0, 0))
    cots = (cot_b, cot_c, send(cot_b, runs, swap), send(cot_c, runs, swap))
    convs = (conv_b, conv_c, send(conv_b, runs, swap), send(conv_c, runs, swap))
    out0, out1, grad0, grad1 = attention(
        convs, cots, norm_gain.reshape(1, chans), w_query, w_key, w_value, w_out
    )
    grad1 = send(grad1, runs, home(0, 1))
    grad0 = send(grad0, runs, home(0, 0))
    out1 = send(out1, runs, home(0, 1))
    out0 = send(out0, runs, home(0, 0))

    for_last, taps = call(
        grad_last_kernel, (grad0, grad1, weight), [VM, VM, VM],
        [((2, block, chans), BF16), ((2, 4, width, 3 * chans), BF16)], [],
        24 * MIB, 10**9,
    )
    handed = lax.ppermute(for_last, "tm", [(i + 1, i) for i in range(runs - 1)])
    own_grad = call(
        grad_own_kernel, (taps, weight, w_last), [VM] * 3, [((2, block, chans), F32)], [],
        24 * MIB, 10**9,
    )[0]
    video_grad, block_out = finish(own_grad, handed, out0, out1)
    return block_out.reshape(video.shape), video_grad.reshape(video.shape)


def solution(mesh):
    spec = P("tm", "rows", None, None)
    return jax.shard_map(
        local,
        mesh=mesh,
        in_specs=(spec, P(), P(), P(), P(), P(), P(), spec),
        out_specs=(spec, spec),
        check_vma=False,
    )
```
